256 devices in a mesh: fsdp: 16 (over z, x_hi), tp: 16 (over x_lo, y, core).
Axes of the slice: x: 4 (x_hi: 2, x_lo: 2; x = x_hi * 2 + x_lo), y: 4, z: 8, core: 2. Of those that a mesh axis runs over, the one named last changes fastest.
Arguments:
- grad_out: bfloat16 [4096, 8192], P('fsdp', 'tp'), may hold values from -6 to 6
- down_q: bfloat16 [14336, 8192], P('fsdp', 'tp'), may hold values from -0.0625 to 0.0625
- scales: bfloat16 [112, 64], P('fsdp', 'tp'), may hold values from 0.25 to 4
- gate_act: bfloat16 [4096, 14336], P('fsdp', 'tp'), may hold values from -6 to 6
- up_act: bfloat16 [4096, 14336], P('fsdp', 'tp'), may hold values from -6 to 6
Outputs:
- grad_gate: bfloat16 [4096, 14336], P('fsdp', 'tp')
- grad_up: bfloat16 [4096, 14336], P('fsdp', 'tp')
The draws below stay inside these ranges and needn't reach their ends.
All inputs are finite; a program needn't handle non-finite values.
Results may differ from the reference program's by a relative error of at most 0.005.
Values may be sent and summed in bfloat16 or wider, within the bound.
No kernel may reach another device: no remote copies, remote signals or barrier semaphores. Data moves between devices by JAX's collectives and lax.ppermute only.
A program may use at most 128 MiB of HBM per device.

```python
import math
import jax
import jax.numpy as jnp
from jax import lax

D = 8192
FF = 14336
BLOCK = 128
TOKENS = 4096


def block_levels(rng, dims, pieces, least, high):
    factor_of, own = 1.0, jax.random.fold_in(rng, 6)
    for axis_at, parts in pieces:
        draws = jnp.exp(jax.random.uniform(jax.random.fold_in(own, axis_at), (parts,), jnp.float32, least / len(pieces), high / len(pieces)))
        factor_of = factor_of * jnp.repeat(draws, dims[axis_at] // parts).reshape([-1 if axis == axis_at else 1 for axis in range(len(dims))])
    return factor_of


def centred(stream_key, dims, width, most, cuts=(), kind=jnp.bfloat16):
    loudness = block_levels(stream_key, dims, cuts, -0.22, 0.18) if cuts else 1.0
    drawn = jax.random.normal(stream_key, dims, jnp.float32) * width * loudness
    return jnp.minimum(jnp.maximum(drawn, -most), most).astype(kind)


def setup_inputs(seed: int = 0) -> dict:
    arg_keys = jax.random.split(jax.random.key(seed), 6)
    grad_out = centred(arg_keys[0], (TOKENS, D), 1.0, 6.0, ((0, 16), (1, 16)))
    down_q = centred(arg_keys[1], (FF, D), D ** -0.5, 0.0625, ((0, 16), (1, 16)))
    scales = jnp.clip(jnp.exp(math.log(4.0) - 2.7725887 * jax.random.uniform(arg_keys[2], (FF // BLOCK, D // BLOCK), jnp.float32) ** block_levels(arg_keys[2], (FF // BLOCK, D // BLOCK), ((0, 16), (1, 16)), -0.2, 0.2)), 0.25, 4.0).astype(jnp.bfloat16)
    gate_act = centred(arg_keys[3], (TOKENS, FF), 1.5, 6.0, ((0, 16), (1, 16)))
    up_act = centred(arg_keys[4], (TOKENS, FF), 1.0, 6.0, ((0, 16), (1, 16)))
    return dict(grad_out=grad_out, down_q=down_q, scales=scales, gate_act=gate_act, up_act=up_act)


def dequantize(values, scales):
    rows, cols = values.shape
    grid = values.astype(jnp.float32).reshape(rows // BLOCK, BLOCK, cols // BLOCK, BLOCK)
    grid = grid * scales.astype(jnp.float32)[:, None, :, None]
    return grid.reshape(rows, cols).astype(jnp.bfloat16)


def reference(grad_out, down_q, scales, gate_act, up_act):
    weight = dequantize(down_q, scales)
    grad_hidden = lax.dot_general(grad_out, weight, (((1,), (1,)), ((), ())), preferred_element_type=jnp.float32)
    gate_val = gate_act.astype(jnp.float32)
    sigmoid_gate = jax.nn.sigmoid(gate_val)
    grad_up = (grad_hidden * gate_val * sigmoid_gate).astype(jnp.bfloat16)
    slope = sigmoid_gate * (1.0 + gate_val * (1.0 - sigmoid_gate))
    grad_gate = (grad_hidden * up_act.astype(jnp.float32) * slope).astype(jnp.bfloat16)
    return grad_gate, grad_up
```

```python
import numpy as np
import jax
import jax.numpy as jnp
from jax import lax
from jax.experimental import pallas as pl
from jax.experimental.pallas import tpu as pltpu
from jax.sharding import Mesh, PartitionSpec as P

BLOCK = 128
Z, XH, XL, Y, C = 8, 2, 2, 4, 2
S = XL * Y
FSDP = ("z", "xh")
TP = ("xl", "y", "c")
ALL = FSDP + TP
BF16, F32 = jnp.bfloat16, jnp.float32

STEP = (0, 2, 4, 6, 1, 3, 5, 7)
PLACE = (0, 1, 3, 5, 6, 7, 4, 2)


def device_index(z, xh, s, c):
    return ((z * XH + xh) * S + s) * C + c


def home_pairs():
    pairs = []
    for z in range(Z):
        sign = 1 if z % 2 == 0 else -1
        for xh in range(XH):
            for s in range(S):
                for c in range(C):
                    to = (z + sign * (STEP[s] + 4 * c)) % Z
                    pairs.append((device_index(z, xh, s, c), device_index(to, xh, z, c)))
    return pairs


def shift(x, axis, size, by):
    return lax.ppermute(x, axis, [(i, (i + by) % size) for i in range(size)])


def dequantize(values, scales):
    rows, cols = values.shape
    grid = values.astype(F32).reshape(rows // BLOCK, BLOCK, cols // BLOCK, BLOCK)
    grid = grid * scales.astype(F32)[:, None, :, None]
    return grid.reshape(rows, cols).astype(BF16)


def product(order, a_own, a_other, w_own, w_other):
    count, rows, depth = a_own.shape
    width = w_own.shape[0]
    dims = (((1,), (1,)), ((), ()))

    def kernel(order_ref, a_own_ref, a_other_ref, w_own_ref, w_other_ref, out_ref):
        total = lax.dot_general(a_own_ref[0], w_own_ref[...], dims, preferred_element_type=F32)
        total += lax.dot_general(a_other_ref[0], w_other_ref[...], dims, preferred_element_type=F32)
        out_ref[0] = total.astype(BF16)

    a_spec = pl.BlockSpec((1, rows, depth), lambda i, order: (order[i], 0, 0))
    w_spec = pl.BlockSpec((width, depth), lambda i, order: (0, 0))
    return pl.pallas_call(
        kernel,
        grid_spec=pltpu.PrefetchScalarGridSpec(
            num_scalar_prefetch=1,
            grid=(count,),
            in_specs=[a_spec, a_spec, w_spec, w_spec],
            out_specs=pl.BlockSpec((1, rows, width), lambda i, order: (i, 0, 0)),
        ),
        out_shape=jax.ShapeDtypeStruct((count, rows, width), BF16),
        compiler_params=pltpu.CompilerParams(vmem_limit_bytes=24 * 2**20),
        cost_estimate=pl.CostEstimate(
            flops=4 * count * rows * depth * width,
            bytes_accessed=2 * (2 * count * rows * depth + 2 * width * depth + count * rows * width),
            transcendentals=0,
        ),
    )(order, a_own, a_other, w_own, w_other)


def on_device(grad_out, down_q, scales, gate_act, up_act):
    z, xh, c = (lax.axis_index(name) for name in ("z", "xh", "c"))

    weight = dequantize(down_q, scales)
    home = xh == c
    at = lambda h, k: h * C + k
    first = lax.ppermute(
        weight, ("xh", "c"), [(at(0, 0), at(1, 0)), (at(1, 1), at(0, 1)), (at(0, 1), at(0, 0)), (at(1, 0), at(1, 1))]
    )
    second = lax.ppermute(weight, ("xh", "c"), [(at(0, 1), at(1, 0)), (at(1, 0), at(0, 1))])
    w_own = jnp.where(home, weight, first)
    w_other = jnp.where(home, first, second)

    half = grad_out.shape[0] // 2
    ahead, behind = [grad_out], [grad_out]
    for _ in range(3):
        behind.append(shift(behind[-1], "z", Z, 1))
        ahead.append(shift(ahead[-1], "z", Z, -1))
    far = jnp.concatenate([shift(behind[3][:half], "z", Z, 1), shift(ahead[3][half:], "z", Z, -1)], 0)
    near_own = jnp.stack([grad_out, ahead[1], behind[1], ahead[2], behind[2]])
    far_own = jnp.stack([ahead[3], far, behind[3]])
    near_other = shift(near_own, "c", C, 1)
    far_other = shift(far_own, "c", C, 1)
    a_own = jnp.concatenate([near_own, far_own], 0)
    a_other = jnp.concatenate([near_other, far_other], 0)

    sign = jnp.where(z % 2 == 0, 1, -1)
    planes = (sign * (jnp.array(STEP, jnp.int32) + 4 * c)) % Z
    order = jnp.array(PLACE, jnp.int32)[planes]

    partial_value = product(order, a_own, a_other, w_own, w_other)
    parts = lax.all_to_all(partial_value, ("xl", "y"), split_axis=0, concat_axis=0, tiled=True)
    summed = parts.astype(F32).sum(0).astype(BF16)
    grad_hidden = lax.ppermute(summed, ALL, home_pairs()).astype(F32)

    gate_val = gate_act.astype(F32)
    sigmoid_gate = jax.nn.sigmoid(gate_val)
    grad_up = (grad_hidden * gate_val * sigmoid_gate).astype(BF16)
    slope = sigmoid_gate * (1.0 + gate_val * (1.0 - sigmoid_gate))
    grad_gate = (grad_hidden * up_act.astype(F32) * slope).astype(BF16)
    return (grad_gate, grad_up)


def solution(mesh):
    fine = Mesh(mesh.devices.reshape(Z, XH, XL, Y, C), ALL)
    spec = P(FSDP, TP)
    return jax.shard_map(
        on_device, mesh=fine, in_specs=(spec,) * 5, out_specs=(spec, spec), check_vma=False
    )
```

```python
import numpy as np
import jax
import jax.numpy as jnp
from jax import lax
from jax.experimental import pallas as pl
from jax.experimental.pallas import tpu as pltpu
from jax.sharding import Mesh, PartitionSpec as P

BLOCK = 128
Z, XH, XL, Y, C = 8, 2, 2, 4, 2
FSDP = ("z", "xh")
TP = ("xl", "y", "c")
ALL = FSDP + TP
BF16, F32 = jnp.bfloat16, jnp.float32
NEAR = 5
PLACE = (0, 1, 3, 5, 6, 7, 4, 2)
CHUNKS = ((0, 512), (512, 384))
VMEM = pl.BlockSpec(memory_space=pltpu.VMEM)
SMEM = pl.BlockSpec(memory_space=pltpu.SMEM)


def device_index(z, xh, s, c):
    return ((z * XH + xh) * XL * Y + s) * C + c


def sign_of(z):
    return 1 if z % 2 == 0 else -1


def home_pairs(j):
    pairs = []
    for z in range(Z):
        for xh in range(XH):
            for xl in range(XL):
                for y in range(Y):
                    for c in range(C):
                        to = (z + sign_of(z) * (y + 4 * (j ^ xl))) % Z
                        pairs.append((device_index(z, xh, xl * Y + y, c), device_index(to, xh, z, c)))
    return pairs


def facts():
    rows = []
    for z in range(Z):
        for xh in range(XH):
            for xl in range(XL):
                for y in range(Y):
                    for c in range(C):
                        row = [PLACE[sign_of(z) * ((y + d) % Y + Y * b) % Z] for d in range(Y) for b in range(2)]
                        source = xl * Y + y
                        away = sign_of(source) * (z - source) % Z
                        rows.append(row + [int(xh == c), xl, away // Y])
    return np.array(rows, np.int32)


def weight_pairs(same, cross):
    at = lambda xh, xl, c: (xh * XL + xl) * C + c
    pairs = []
    for xh in range(XH):
        for xl in range(XL):
            for c in range(C):
                a, b = same if xh == c else cross
                pairs.append((at(xh, xl, c), at(xh ^ a, xl ^ b, xh)))
    return pairs


def shift(x, axis, size, by):
    return lax.ppermute(x, axis, [(i, (i + by) % size) for i in range(size)])


def dequantize(values, scales):
    rows, cols = values.shape
    grid = values.astype(F32).reshape(rows // BLOCK, BLOCK, cols // BLOCK, BLOCK)
    grid = grid * scales.astype(F32)[:, None, :, None]
    return grid.reshape(rows, cols).astype(BF16)


def product(own, stacks, weights, start, width):
    rows, depth = stacks[0].shape[1:]
    half = depth // 2
    dims = (((1,), (1,)), ((), ()))

    def kernel(facts_ref, near_own, far_own, near_other, far_other, *refs):
        w_refs, out_refs, (first, second) = refs[:4], refs[4 : 4 + Y], refs[4 + Y :]
        home = facts_ref[2 * Y]
        for d in range(Y):
            for b in range(2):
                slot = facts_ref[2 * d + b]
                here = slice(b * rows, (b + 1) * rows)
                for at_home, one, two in ((1, (near_own, far_own), (near_other, far_other)), (0, (near_other, far_other), (near_own, far_own))):

                    @pl.when((home == at_home) & (slot < NEAR))
                    def _():
                        first[here, :] = one[0][slot]
                        second[here, :] = two[0][slot]

                    @pl.when((home == at_home) & (slot >= NEAR))
                    def _():
                        first[here, :] = one[1][slot - NEAR]
                        second[here, :] = two[1][slot - NEAR]

            total = None
            for lhs, k, w in ((first, 0, 0), (second, 0, 1), (second, 1, 2), (first, 1, 3)):
                term = lax.dot_general(
                    lhs[:, k * half : (k + 1) * half],
                    w_refs[w][start : start + width, :],
                    dims,
                    preferred_element_type=F32,
                )
                total = term if total is None else total + term
            total = total.astype(BF16)
            out_refs[d][0] = total[:rows]
            out_refs[d][1] = total[rows:]

    return pl.pallas_call(
        kernel,
        in_specs=[SMEM] + [VMEM] * 8,
        out_specs=[VMEM] * Y,
        out_shape=[jax.ShapeDtypeStruct((2, rows, width), BF16)] * Y,
        scratch_shapes=[pltpu.VMEM((2 * rows, depth), BF16)] * 2,
        compiler_params=pltpu.CompilerParams(vmem_limit_bytes=32 * 2**20),
        cost_estimate=pl.CostEstimate(
            flops=2 * 2 * Y * rows * 2 * depth * width, bytes_accessed=10 * 2**20, transcendentals=0
        ),
    )(own, *stacks, *weights)


def add_up(own, parts):
    _, rows, width = parts[0].shape

    def kernel(facts_ref, *refs):
        for j in range(2):
            b = jnp.where(facts_ref[2 * Y + 1] == 0, j, 1 - j)
            total = refs[0][b].astype(F32)
            for ref in refs[1:Y]:
                total += ref[b].astype(F32)
            refs[Y + j][...] = total.astype(BF16)

    return pl.pallas_call(
        kernel,
        in_specs=[SMEM] + [VMEM] * Y,
        out_specs=[VMEM] * 2,
        out_shape=[jax.ShapeDtypeStruct((rows, width), BF16)] * 2,
        compiler_params=pltpu.CompilerParams(vmem_limit_bytes=16 * 2**20),
        cost_estimate=pl.CostEstimate(flops=2 * Y * rows * width, bytes_accessed=4 * (Y + 1) * rows * width, transcendentals=0),
    )(own, *parts)


def swiglu_backward(own, hidden, gate_act, up_act):
    rows, width = gate_act.shape
    half = rows // 2

    def kernel(facts_ref, *refs):
        gate_ref, up_ref, grad_gate_ref, grad_up_ref = refs[4:]
        flip = facts_ref[2 * Y + 2] == 1
        for i, (start, count) in enumerate(CHUNKS):
            columns = slice(start, start + count)
            for h in range(2):
                here = slice(h * half, (h + 1) * half)
                value = jnp.where(flip, refs[2 * i + 1 - h][...].astype(F32), refs[2 * i + h][...].astype(F32))
                gate = gate_ref[here, columns].astype(F32)
                sigmoid = jax.nn.sigmoid(gate)
                grad_up_ref[here, columns] = (value * gate * sigmoid).astype(BF16)
                slope = sigmoid * (1.0 + gate * (1.0 - sigmoid))
                grad_gate_ref[here, columns] = (value * up_ref[here, columns].astype(F32) * slope).astype(BF16)

    shape = jax.ShapeDtypeStruct((rows, width), BF16)
    return pl.pallas_call(
        kernel,
        in_specs=[SMEM] + [VMEM] * 6,
        out_specs=[VMEM] * 2,
        out_shape=[shape] * 2,
        compiler_params=pltpu.CompilerParams(vmem_limit_bytes=16 * 2**20),
        cost_estimate=pl.CostEstimate(flops=10 * rows * width, bytes_accessed=10 * rows * width, transcendentals=rows * width),
    )(own, *[x for chunk in hidden for x in chunk], gate_act, up_act)


def on_device(grad_out, down_q, scales, gate_act, up_act):
    xl, c = lax.axis_index("xl"), lax.axis_index("c")

    rows = grad_out.shape[0] // 2
    mine = lax.dynamic_slice_in_dim(grad_out, xl * rows, rows, 0)
    theirs = lax.dynamic_slice_in_dim(grad_out, (1 - xl) * rows, rows, 0)
    tokens = jnp.concatenate([mine, shift(theirs, "xl", XL, 1)], 1)

    weight = dequantize(down_q, scales)
    rounds = (((0, 0), (1, 0)), ((1, 0), (0, 0)), ((1, 1), (0, 1)), ((0, 1), (1, 1)))
    weights = [lax.ppermute(weight, ("xh", "xl", "c"), weight_pairs(*pair)) for pair in rounds]

    ahead, behind = [tokens], [tokens]
    for _ in range(3):
        behind.append(shift(behind[-1], "z", Z, 1))
        ahead.append(shift(ahead[-1], "z", Z, -1))
    around = [(i * C, (i + 1) % Z * C) for i in range(Z)] + [(i * C + 1, (i - 1) % Z * C + 1) for i in range(Z)]
    far = lax.ppermute(jnp.where(c == 0, behind[3], ahead[3]), ("z", "c"), around)
    near_own = jnp.stack([tokens, ahead[1], behind[1], ahead[2], behind[2]])
    far_own = jnp.stack([ahead[3], far, behind[3]])
    stacks = (near_own, far_own, shift(near_own, "c", C, 1), shift(far_own, "c", C, 1))

    own = lax.dynamic_index_in_dim(jnp.asarray(facts()), lax.axis_index(ALL), 0, keepdims=False)
    hidden = []
    for start, width in CHUNKS:
        outs = product(own, stacks, weights, start, width)
        parts = [outs[0]] + [shift(outs[d], "y", Y, d) for d in range(1, Y)]
        sums = add_up(own, parts)
        hidden.append([lax.ppermute(sums[j], ALL, home_pairs(j)) for j in range(2)])

    return tuple(swiglu_backward(own, hidden, gate_act, up_act))


def solution(mesh):
    fine = Mesh(mesh.devices.reshape(Z, XH, XL, Y, C), ALL)
    spec = P(FSDP, TP)
    return jax.shard_map(
        on_device, mesh=fine, in_specs=(spec,) * 5, out_specs=(spec, spec), check_vma=False
    )
```

```python
import numpy as np
import jax
import jax.numpy as jnp
from jax import lax
from jax.experimental import pallas as pl
from jax.experimental.pallas import tpu as pltpu
from jax.sharding import Mesh, PartitionSpec as P

BLOCK = 128
Z, XH, XL, Y, C = 8, 2, 2, 4, 2
S = XL * Y
FSDP = ("z", "xh")
TP = ("xl", "y", "c")
ALL = FSDP + TP
BF16, F32 = jnp.bfloat16, jnp.float32
VMEM = pl.BlockSpec(memory_space=pltpu.VMEM)
SMEM = pl.BlockSpec(memory_space=pltpu.SMEM)

TURN = (0, 2, 4, 6, 1, 3, 5, 7)


def number_of(z, s):
    return TURN[s] if z % 2 == 0 else 7 - TURN[s]


def half_of(number, c):
    return c if number in (0, 7) else (number - 1) % 2


def device_index(z, xh, s, c):
    return ((z * XH + xh) * S + s) * C + c


def home_pairs(j):
    pairs = []
    for z in range(Z):
        for xh in range(XH):
            for s in range(S):
                for c in range(C):
                    number = number_of(z, s)
                    away = (number + 1) // 2
                    to = (z - away if c == 0 else z + away) % Z
                    pairs.append((device_index(z, xh, s, c), device_index(to, xh, z, j ^ half_of(number, c))))
    return pairs


def facts():
    rows = []
    for z in range(Z):
        for xh in range(XH):
            for xl in range(XL):
                for y in range(Y):
                    for c in range(C):
                        place = [0] * S
                        for s in range(S):
                            place[number_of(z, s)] = 2 * ((s % Y - y) % Y) + ((s // Y) ^ xl)
                        rows.append(place + [c, half_of(number_of(z, xl * Y + y), c) ^ xh])
    return np.array(rows, np.int32)


def shift(x, axis, size, by):
    return lax.ppermute(x, axis, [(i, (i + by) % size) for i in range(size)])


def dequantize(values, scales):
    rows, cols = values.shape
    grid = values.astype(F32).reshape(rows // BLOCK, BLOCK, cols // BLOCK, BLOCK)
    grid = grid * scales.astype(F32)[:, None, :, None]
    return grid.reshape(rows, cols).astype(BF16)


DIMS = (((1,), (1,)), ((), ()))


def times(lhs, w_own, w_other):
    half = lhs.shape[1] // 2
    total = lax.dot_general(lhs[:, :half], w_own, DIMS, preferred_element_type=F32)
    total += lax.dot_general(lhs[:, half:], w_other, DIMS, preferred_element_type=F32)
    return total.astype(BF16)


def params(mib):
    return pltpu.CompilerParams(vmem_limit_bytes=mib * 2**20)


def product_xl(own, tokens, far, w_own, w_other):
    rows, depth = far.shape
    width = w_own.shape[0]

    def kernel(facts_ref, t0, t1, t2, t3, far_ref, w_own_ref, w_other_ref, lhs_ref, keep_ref, send_ref):
        lhs_ref[facts_ref[0]] = t0[pl.ds(pl.multiple_of(facts_ref[S] * rows, rows), rows), :]
        for i, ref in enumerate((t1, t2, t3)):
            for h in range(2):
                lhs_ref[facts_ref[1 + 2 * i + h]] = ref[h * rows : (h + 1) * rows, :]
        lhs_ref[facts_ref[7]] = far_ref[...]
        for d in range(Y):
            pair = lhs_ref[2 * d : 2 * d + 2].reshape(2 * rows, depth)
            total = times(pair, w_own_ref[...], w_other_ref[...])
            keep_ref[d] = total[:rows]
            send_ref[d] = total[rows:]

    part = jax.ShapeDtypeStruct((Y, rows, width), BF16)
    return pl.pallas_call(
        kernel,
        in_specs=[SMEM] + [VMEM] * 7,
        out_specs=[VMEM] * 3,
        out_shape=[jax.ShapeDtypeStruct((S, rows, depth), BF16), part, part],
        compiler_params=params(32),
        cost_estimate=pl.CostEstimate(flops=2 * S * rows * depth * width, bytes_accessed=8 * 2**20, transcendentals=0),
    )(own, *tokens, far, w_own, w_other)


def product_y(lhs, w_own, w_other):
    _, rows, depth = lhs.shape
    width = w_own.shape[0]

    def kernel(lhs_ref, w_own_ref, w_other_ref, *out_refs):
        for d in range(Y):
            pair = lhs_ref[2 * d : 2 * d + 2].reshape(2 * rows, depth)
            total = times(pair, w_own_ref[...], w_other_ref[...])
            out_refs[d][0] = total[:rows]
            out_refs[d][1] = total[rows:]

    return pl.pallas_call(
        kernel,
        in_specs=[VMEM] * 3,
        out_specs=[VMEM] * Y,
        out_shape=[jax.ShapeDtypeStruct((2, rows, width), BF16)] * Y,
        compiler_params=params(32),
        cost_estimate=pl.CostEstimate(flops=2 * S * rows * depth * width, bytes_accessed=6 * 2**20, transcendentals=0),
    )(lhs, w_own, w_other)


def add_y(parts):
    _, rows, width = parts[0].shape

    def kernel(*refs):
        for e in range(2):
            total = refs[0][e].astype(F32)
            for ref in refs[1:Y]:
                total += ref[e].astype(F32)
            refs[Y + e][...] = total.astype(BF16)

    return pl.pallas_call(
        kernel,
        in_specs=[VMEM] * Y,
        out_specs=[VMEM] * 2,
        out_shape=[jax.ShapeDtypeStruct((rows, width), BF16)] * 2,
        compiler_params=params(16),
        cost_estimate=pl.CostEstimate(flops=2 * Y * rows * width, bytes_accessed=4 * (Y + 1) * rows * width, transcendentals=0),
    )(*parts)


def add_xl(kept, received):
    _, rows, width = kept.shape

    def kernel(kept_ref, received_ref, *out_refs):
        for d in range(Y):
            out_refs[d][...] = (kept_ref[d].astype(F32) + received_ref[d].astype(F32)).astype(BF16)

    return pl.pallas_call(
        kernel,
        in_specs=[VMEM] * 2,
        out_specs=[VMEM] * Y,
        out_shape=[jax.ShapeDtypeStruct((rows, width), BF16)] * Y,
        compiler_params=params(16),
        cost_estimate=pl.CostEstimate(flops=Y * rows * width, bytes_accessed=6 * Y * rows * width, transcendentals=0),
    )(kept, received)


def add_last(own, near_parts, cross_parts):
    rows, width = near_parts[0].shape
    count = len(near_parts)

    def kernel(facts_ref, *refs):
        sums = []
        for parts in (refs[:count], refs[count : count + Y]):
            total = parts[0][...].astype(F32)
            for ref in parts[1:]:
                total += ref[...].astype(F32)
            sums.append(total)
        straight = facts_ref[S + 1] == 0
        refs[count + Y][...] = jnp.where(straight, sums[0], sums[1]).astype(BF16)
        refs[count + Y + 1][...] = jnp.where(straight, sums[1], sums[0]).astype(BF16)

    return pl.pallas_call(
        kernel,
        in_specs=[SMEM] + [VMEM] * (count + Y),
        out_specs=[VMEM] * 2,
        out_shape=[jax.ShapeDtypeStruct((rows, width), BF16)] * 2,
        compiler_params=params(16),
        cost_estimate=pl.CostEstimate(flops=8 * rows * width, bytes_accessed=16 * rows * width, transcendentals=0),
    )(own, *near_parts, *cross_parts)


def swiglu_backward(own, hidden, gate_act, up_act):
    rows, width = gate_act.shape
    half = rows // 2

    def kernel(facts_ref, first, second, gate_ref, up_ref, grad_gate_ref, grad_up_ref):
        flip = facts_ref[S] == 1
        for h, (straight, crossed) in enumerate(((first, second), (second, first))):
            here = slice(h * half, (h + 1) * half)
            value = jnp.where(flip, crossed[...].astype(F32), straight[...].astype(F32))
            gate = gate_ref[here, :].astype(F32)
            sigmoid = jax.nn.sigmoid(gate)
            grad_up_ref[here, :] = (value * gate * sigmoid).astype(BF16)
            slope = sigmoid * (1.0 + gate * (1.0 - sigmoid))
            grad_gate_ref[here, :] = (value * up_ref[here, :].astype(F32) * slope).astype(BF16)

    return pl.pallas_call(
        kernel,
        in_specs=[SMEM] + [VMEM] * 4,
        out_specs=[VMEM] * 2,
        out_shape=[jax.ShapeDtypeStruct((rows, width), BF16)] * 2,
        compiler_params=params(16),
        cost_estimate=pl.CostEstimate(flops=10 * rows * width, bytes_accessed=10 * rows * width, transcendentals=rows * width),
    )(own, *hidden, gate_act, up_act)


def on_device(grad_out, down_q, scales, gate_act, up_act):
    c = lax.axis_index("c")
    own = lax.dynamic_index_in_dim(jnp.asarray(facts()), lax.axis_index(ALL), 0, keepdims=False)

    rows = grad_out.shape[0] // 2
    tokens = [jnp.concatenate([grad_out, shift(grad_out, "c", C, 1)], 1)]
    around = [(i * C, (i + 1) % Z * C) for i in range(Z)] + [(i * C + 1, (i - 1) % Z * C + 1) for i in range(Z)]
    for _ in range(3):
        tokens.append(lax.ppermute(tokens[-1], ("z", "c"), around))
    far = lax.ppermute(lax.dynamic_slice_in_dim(tokens[3], c * rows, rows, 0), ("z", "c"), around)

    near_own = dequantize(down_q, scales)
    cross_own = shift(near_own, "xh", XH, 1)
    near_other = shift(near_own, "c", C, 1)
    late, _ = lax.optimization_barrier((cross_own, tokens[3]))
    cross_other = shift(late, "c", C, 1)

    lhs, kept, sent = product_xl(own, tokens, far, cross_own, cross_other)
    cross = add_xl(kept, shift(sent, "xl", XL, 1))
    cross_parts = [cross[0]] + [shift(cross[d], "y", Y, d) for d in range(1, Y)]

    near = product_y(lhs, near_own, near_other)
    kept, sent = add_y([near[0]] + [shift(near[d], "y", Y, d) for d in range(1, Y)])
    near_parts = [kept, shift(sent, "xl", XL, 1)]

    sums = add_last(own, near_parts, cross_parts)
    hidden = [lax.ppermute(sums[j], ALL, home_pairs(j)) for j in range(2)]
    return tuple(swiglu_backward(own, hidden, gate_act, up_act))


def solution(mesh):
    fine = Mesh(mesh.devices.reshape(Z, XH, XL, Y, C), ALL)
    spec = P(FSDP, TP)
    return jax.shard_map(
        on_device, mesh=fine, in_specs=(spec,) * 5, out_specs=(spec, spec), check_vma=False
    )
```

```python
import numpy as np
import jax
import jax.numpy as jnp
from jax import lax
from jax.experimental import pallas as pl
from jax.experimental.pallas import tpu as pltpu
from jax.sharding import Mesh, PartitionSpec as P

BLOCK = 128
Z, XH, XL, Y, C = 8, 2, 2, 4, 2
S = XL * Y
FSDP = ("z", "xh")
TP = ("xl", "y", "c")
ALL = FSDP + TP
BF16, F32 = jnp.bfloat16, jnp.float32
VMEM = pl.BlockSpec(memory_space=pltpu.VMEM)
SMEM = pl.BlockSpec(memory_space=pltpu.SMEM)

NUMBER = (
    ((2, 5, 6, 1, 4, 0, 3, 7), (7, 3, 2, 4, 6, 1, 5, 0)),
    ((0, 5, 4, 6, 1, 7, 2, 3), (7, 3, 1, 4, 2, 5, 6, 0)),
    ((4, 2, 7, 0, 6, 1, 5, 3), (7, 5, 1, 4, 3, 2, 0, 6)),
    ((1, 5, 6, 4, 3, 7, 2, 0), (0, 5, 2, 1, 4, 6, 3, 7)),
    ((6, 4, 1, 7, 3, 0, 5, 2), (1, 0, 7, 4, 6, 2, 5, 3)),
    ((1, 3, 2, 7, 4, 6, 0, 5), (4, 6, 7, 0, 1, 3, 2, 5)),
    ((5, 4, 2, 6, 1, 0, 3, 7), (7, 5, 2, 1, 6, 4, 3, 0)),
    ((1, 0, 2, 4, 5, 7, 6, 3), (1, 0, 6, 4, 2, 5, 3, 7)),
)


def number_of(z, s, c):
    return NUMBER[z][c][s]


def half_of(number, c):
    return c if number in (0, 7) else (number - 1) % 2


def device_index(z, xh, s, c):
    return ((z * XH + xh) * S + s) * C + c


def home_pairs(j):
    pairs = []
    for z in range(Z):
        for xh in range(XH):
            for s in range(S):
                for c in range(C):
                    number = number_of(z, s, c)
                    away = (number + 1) // 2
                    to = (z - away if c == 0 else z + away) % Z
                    pairs.append((device_index(z, xh, s, c), device_index(to, xh, z, j ^ half_of(number, c))))
    return pairs


def facts():
    rows = []
    for z in range(Z):
        for xh in range(XH):
            for xl in range(XL):
                for y in range(Y):
                    for c in range(C):
                        place = [0] * S
                        for s in range(S):
                            place[number_of(z, s, c)] = 2 * ((s % Y - y) % Y) + ((s // Y) ^ xl)
                        rows.append(place + [c, half_of(number_of(z, xl * Y + y, c), c) ^ xh])
    return np.array(rows, np.int32)


def shift(x, axis, size, by):
    return lax.ppermute(x, axis, [(i, (i + by) % size) for i in range(size)])


def dequantize(values, scales):
    rows, cols = values.shape
    grid = values.astype(F32).reshape(rows // BLOCK, BLOCK, cols // BLOCK, BLOCK)
    grid = grid * scales.astype(F32)[:, None, :, None]
    return grid.reshape(rows, cols).astype(BF16)


DIMS = (((1,), (1,)), ((), ()))


def times(lhs, w_own, w_other):
    half = lhs.shape[1] // 2
    total = lax.dot_general(lhs[:, :half], w_own, DIMS, preferred_element_type=F32)
    total += lax.dot_general(lhs[:, half:], w_other, DIMS, preferred_element_type=F32)
    return total.astype(BF16)


def params(mib):
    return pltpu.CompilerParams(vmem_limit_bytes=mib * 2**20)


def product_y(own, tokens, far, w_own, w_other):
    rows, depth = far.shape
    width = w_own.shape[0]

    def kernel(facts_ref, t0, t1, t2, t3, far_ref, w_own_ref, w_other_ref, lhs_ref, *out_refs):
        lhs_ref[facts_ref[0]] = t0[pl.ds(pl.multiple_of(facts_ref[S] * rows, rows), rows), :]
        for i, ref in enumerate((t1, t2, t3)):
            for h in range(2):
                lhs_ref[facts_ref[1 + 2 * i + h]] = ref[h * rows : (h + 1) * rows, :]
        lhs_ref[facts_ref[7]] = far_ref[...]
        for d in range(Y):
            pair = lhs_ref[2 * d : 2 * d + 2].reshape(2 * rows, depth)
            total = times(pair, w_own_ref[...], w_other_ref[...])
            out_refs[d][0] = total[:rows]
            out_refs[d][1] = total[rows:]

    return pl.pallas_call(
        kernel,
        in_specs=[SMEM] + [VMEM] * 7,
        out_specs=[VMEM] * (1 + Y),
        out_shape=[jax.ShapeDtypeStruct((S, rows, depth), BF16)]
        + [jax.ShapeDtypeStruct((2, rows, width), BF16)] * Y,
        compiler_params=params(32),
        cost_estimate=pl.CostEstimate(flops=2 * S * rows * depth * width, bytes_accessed=8 * 2**20, transcendentals=0),
    )(own, *tokens, far, w_own, w_other)


def product_xl(lhs, w_own, w_other):
    _, rows, depth = lhs.shape
    width = w_own.shape[0]

    def kernel(lhs_ref, w_own_ref, w_other_ref, keep_ref, send_ref):
        for d in range(Y):
            pair = lhs_ref[2 * d : 2 * d + 2].reshape(2 * rows, depth)
            total = times(pair, w_own_ref[...], w_other_ref[...])
            keep_ref[d] = total[:rows]
            send_ref[d] = total[rows:]

    return pl.pallas_call(
        kernel,
        in_specs=[VMEM] * 3,
        out_specs=[VMEM] * 2,
        out_shape=[jax.ShapeDtypeStruct((Y, rows, width), BF16)] * 2,
        compiler_params=params(32),
        cost_estimate=pl.CostEstimate(flops=2 * S * rows * depth * width, bytes_accessed=6 * 2**20, transcendentals=0),
    )(lhs, w_own, w_other)


def add_y(parts):
    _, rows, width = parts[0].shape

    def kernel(*refs):
        for e in range(2):
            total = refs[0][e].astype(F32)
            for ref in refs[1:Y]:
                total += ref[e].astype(F32)
            refs[Y + e][...] = total.astype(BF16)

    return pl.pallas_call(
        kernel,
        in_specs=[VMEM] * Y,
        out_specs=[VMEM] * 2,
        out_shape=[jax.ShapeDtypeStruct((rows, width), BF16)] * 2,
        compiler_params=params(16),
        cost_estimate=pl.CostEstimate(flops=2 * Y * rows * width, bytes_accessed=4 * (Y + 1) * rows * width, transcendentals=0),
    )(*parts)


def add_xl(kept, received):
    _, rows, width = kept.shape

    def kernel(kept_ref, received_ref, *out_refs):
        for d in range(Y):
            out_refs[d][...] = (kept_ref[d].astype(F32) + received_ref[d].astype(F32)).astype(BF16)

    return pl.pallas_call(
        kernel,
        in_specs=[VMEM] * 2,
        out_specs=[VMEM] * Y,
        out_shape=[jax.ShapeDtypeStruct((rows, width), BF16)] * Y,
        compiler_params=params(16),
        cost_estimate=pl.CostEstimate(flops=Y * rows * width, bytes_accessed=6 * Y * rows * width, transcendentals=0),
    )(kept, received)


def add_last(own, near_parts, cross_parts):
    rows, width = near_parts[0].shape
    count = len(near_parts)

    def kernel(facts_ref, *refs):
        sums = []
        for parts in (refs[:count], refs[count : count + Y]):
            total = parts[0][...].astype(F32)
            for ref in parts[1:]:
                total += ref[...].astype(F32)
            sums.append(total)
        straight = facts_ref[S + 1] == 0
        refs[count + Y][...] = jnp.where(straight, sums[0], sums[1]).astype(BF16)
        refs[count + Y + 1][...] = jnp.where(straight, sums[1], sums[0]).astype(BF16)

    return pl.pallas_call(
        kernel,
        in_specs=[SMEM] + [VMEM] * (count + Y),
        out_specs=[VMEM] * 2,
        out_shape=[jax.ShapeDtypeStruct((rows, width), BF16)] * 2,
        compiler_params=params(16),
        cost_estimate=pl.CostEstimate(flops=8 * rows * width, bytes_accessed=16 * rows * width, transcendentals=0),
    )(own, *near_parts, *cross_parts)


def swiglu_backward(own, hidden, gate_act, up_act):
    rows, width = gate_act.shape
    half = rows // 2

    def kernel(facts_ref, first, second, gate_ref, up_ref, grad_gate_ref, grad_up_ref):
        flip = facts_ref[S] == 1
        for h, (straight, crossed) in enumerate(((first, second), (second, first))):
            here = slice(h * half, (h + 1) * half)
            value = jnp.where(flip, crossed[...].astype(F32), straight[...].astype(F32))
            gate = gate_ref[here, :].astype(F32)
            sigmoid = jax.nn.sigmoid(gate)
            grad_up_ref[here, :] = (value * gate * sigmoid).astype(BF16)
            slope = sigmoid * (1.0 + gate * (1.0 - sigmoid))
            grad_gate_ref[here, :] = (value * up_ref[here, :].astype(F32) * slope).astype(BF16)

    return pl.pallas_call(
        kernel,
        in_specs=[SMEM] + [VMEM] * 4,
        out_specs=[VMEM] * 2,
        out_shape=[jax.ShapeDtypeStruct((rows, width), BF16)] * 2,
        compiler_params=params(16),
        cost_estimate=pl.CostEstimate(flops=10 * rows * width, bytes_accessed=10 * rows * width, transcendentals=rows * width),
    )(own, *hidden, gate_act, up_act)


def on_device(grad_out, down_q, scales, gate_act, up_act):
    c = lax.axis_index("c")
    own = lax.dynamic_index_in_dim(jnp.asarray(facts()), lax.axis_index(ALL), 0, keepdims=False)

    near_own = dequantize(down_q, scales)
    cross_own = shift(near_own, "xh", XH, 1)

    rows = grad_out.shape[0] // 2
    tokens = [jnp.concatenate([grad_out, shift(grad_out, "c", C, 1)], 1)]
    around = [(i * C, (i + 1) % Z * C) for i in range(Z)] + [(i * C + 1, (i - 1) % Z * C + 1) for i in range(Z)]
    for step in range(3):
        if step == 2:
            tokens[-1], cross_own = lax.optimization_barrier((tokens[-1], cross_own))
        tokens.append(lax.ppermute(tokens[-1], ("z", "c"), around))
    far = lax.ppermute(lax.dynamic_slice_in_dim(tokens[3], c * rows, rows, 0), ("z", "c"), around)
    near_other = shift(near_own, "c", C, 1)
    cross_other = shift(cross_own, "c", C, 1)

    lhs, *near = product_y(own, tokens, far, near_own, near_other)
    near_y = [near[0]] + [shift(near[d], "y", Y, d) for d in range(1, Y)]
    kept, sent = product_xl(lhs, cross_own, cross_other)
    cross = add_xl(kept, shift(sent, "xl", XL, 1))
    cross_parts = [cross[0]] + [shift(cross[d], "y", Y, d) for d in range(1, Y)]
    kept, sent = add_y(near_y)
    near_parts = [kept, shift(sent, "xl", XL, 1)]

    sums = add_last(own, near_parts, cross_parts)
    hidden = [lax.ppermute(sums[j], ALL, home_pairs(j)) for j in range(2)]
    return tuple(swiglu_backward(own, hidden, gate_act, up_act))


def solution(mesh):
    fine = Mesh(mesh.devices.reshape(Z, XH, XL, Y, C), ALL)
    spec = P(FSDP, TP)
    return jax.shard_map(
        on_device, mesh=fine, in_specs=(spec,) * 5, out_specs=(spec, spec), check_vma=False
    )
```

```python
import numpy as np
import jax
import jax.numpy as jnp
from jax import lax
from jax.experimental import pallas as pl
from jax.experimental.pallas import tpu as pltpu
from jax.sharding import Mesh, PartitionSpec as P

BLOCK = 128
Z, XH, XL, Y, C = 8, 2, 2, 4, 2
S = XL * Y
FSDP = ("z", "xh")
TP = ("xl", "y", "c")
ALL = FSDP + TP
BF16, F32 = jnp.bfloat16, jnp.float32
VMEM = pl.BlockSpec(memory_space=pltpu.VMEM)
SMEM = pl.BlockSpec(memory_space=pltpu.SMEM)

NUMBER = (
    ((2, 5, 6, 1, 4, 0, 3, 7), (7, 3, 2, 4, 6, 1, 5, 0)),
    ((0, 5, 4, 6, 1, 7, 2, 3), (7, 3, 1, 4, 2, 5, 6, 0)),
    ((4, 2, 7, 0, 6, 1, 5, 3), (7, 5, 1, 4, 3, 2, 0, 6)),
    ((1, 5, 6, 4, 3, 7, 2, 0), (0, 5, 2, 1, 4, 6, 3, 7)),
    ((6, 4, 1, 7, 3, 0, 5, 2), (1, 0, 7, 4, 6, 2, 5, 3)),
    ((1, 3, 2, 7, 4, 6, 0, 5), (4, 6, 7, 0, 1, 3, 2, 5)),
    ((5, 4, 2, 6, 1, 0, 3, 7), (7, 5, 2, 1, 6, 4, 3, 0)),
    ((1, 0, 2, 4, 5, 7, 6, 3), (1, 0, 6, 4, 2, 5, 3, 7)),
)


def number_of(z, s, c):
    return NUMBER[z][c][s]


def half_of(number, c):
    return c if number in (0, 7) else (number - 1) % 2


def device_index(z, xh, s, c):
    return ((z * XH + xh) * S + s) * C + c


def home_pairs(j):
    pairs = []
    for z in range(Z):
        for xh in range(XH):
            for s in range(S):
                for c in range(C):
                    number = number_of(z, s, c)
                    away = (number + 1) // 2
                    to = (z - away if c == 0 else z + away) % Z
                    pairs.append((device_index(z, xh, s, c), device_index(to, xh, z, j ^ half_of(number, c))))
    return pairs


def facts():
    rows = []
    for z in range(Z):
        for xh in range(XH):
            for xl in range(XL):
                for y in range(Y):
                    for c in range(C):
                        place = [0] * S
                        for s in range(S):
                            place[number_of(z, s, c)] = 2 * ((s % Y - y) % Y) + ((s // Y) ^ xl)
                        rows.append(place + [c, half_of(number_of(z, xl * Y + y, c), c) ^ xh])
    return np.array(rows, np.int32)


def shift(x, axis, size, by):
    return lax.ppermute(x, axis, [(i, (i + by) % size) for i in range(size)])


def dequantize(values, scales):
    rows, cols = values.shape
    grid = values.astype(F32).reshape(rows // BLOCK, BLOCK, cols // BLOCK, BLOCK)
    grid = grid * scales.astype(F32)[:, None, :, None]
    return grid.reshape(rows, cols).astype(BF16)


DIMS = (((1,), (1,)), ((), ()))


def times(lhs, w_own, w_other):
    half = lhs.shape[1] // 2
    total = lax.dot_general(lhs[:, :half], w_own, DIMS, preferred_element_type=F32)
    total += lax.dot_general(lhs[:, half:], w_other, DIMS, preferred_element_type=F32)
    return total.astype(BF16)


def params(mib):
    return pltpu.CompilerParams(vmem_limit_bytes=mib * 2**20)


def product_y(own, tokens, far, w_own, w_other):
    rows, depth = far.shape
    width = w_own.shape[0]

    def kernel(facts_ref, t0, t1, t2, t3, far_ref, w_own_ref, w_other_ref, lhs_ref, *out_refs):
        lhs_ref[facts_ref[0]] = t0[pl.ds(pl.multiple_of(facts_ref[S] * rows, rows), rows), :]
        for i, ref in enumerate((t1, t2, t3)):
            for h in range(2):
                lhs_ref[facts_ref[1 + 2 * i + h]] = ref[h * rows : (h + 1) * rows, :]
        lhs_ref[facts_ref[7]] = far_ref[...]
        for d in range(Y):
            pair = lhs_ref[2 * d : 2 * d + 2].reshape(2 * rows, depth)
            total = times(pair, w_own_ref[...], w_other_ref[...])
            out_refs[d][0] = total[:rows]
            out_refs[d][1] = total[rows:]

    return pl.pallas_call(
        kernel,
        in_specs=[SMEM] + [VMEM] * 7,
        out_specs=[VMEM] * (1 + Y),
        out_shape=[jax.ShapeDtypeStruct((S, rows, depth), BF16)]
        + [jax.ShapeDtypeStruct((2, rows, width), BF16)] * Y,
        compiler_params=params(32),
        cost_estimate=pl.CostEstimate(flops=2 * S * rows * depth * width, bytes_accessed=8 * 2**20, transcendentals=0),
    )(own, *tokens, far, w_own, w_other)


def product_xl(lhs, w_own, w_other):
    _, rows, depth = lhs.shape
    width = w_own.shape[0]

    def kernel(lhs_ref, w_own_ref, w_other_ref, keep_ref, *send_refs):
        for d in range(Y):
            pair = lhs_ref[2 * d : 2 * d + 2].reshape(2 * rows, depth)
            total = times(pair, w_own_ref[...], w_other_ref[...])
            keep_ref[d] = total[:rows]
            send_refs[d // 2][d % 2] = total[rows:]

    return pl.pallas_call(
        kernel,
        in_specs=[VMEM] * 3,
        out_specs=[VMEM] * 3,
        out_shape=[jax.ShapeDtypeStruct((n, rows, width), BF16) for n in (Y, Y // 2, Y // 2)],
        compiler_params=params(32),
        cost_estimate=pl.CostEstimate(flops=2 * S * rows * depth * width, bytes_accessed=6 * 2**20, transcendentals=0),
    )(lhs, w_own, w_other)


def add_y(parts):
    _, rows, width = parts[0].shape

    def kernel(*refs):
        for e in range(2):
            total = refs[0][e].astype(F32)
            for ref in refs[1:Y]:
                total += ref[e].astype(F32)
            refs[Y + e][...] = total.astype(BF16)

    return pl.pallas_call(
        kernel,
        in_specs=[VMEM] * Y,
        out_specs=[VMEM] * 2,
        out_shape=[jax.ShapeDtypeStruct((rows, width), BF16)] * 2,
        compiler_params=params(16),
        cost_estimate=pl.CostEstimate(flops=2 * Y * rows * width, bytes_accessed=4 * (Y + 1) * rows * width, transcendentals=0),
    )(*parts)


def add_xl(kept, received):
    _, rows, width = kept.shape

    def kernel(kept_ref, low_ref, high_ref, *out_refs):
        for d in range(Y):
            received = (low_ref, high_ref)[d // 2][d % 2]
            out_refs[d][...] = (kept_ref[d].astype(F32) + received.astype(F32)).astype(BF16)

    return pl.pallas_call(
        kernel,
        in_specs=[VMEM] * 3,
        out_specs=[VMEM] * Y,
        out_shape=[jax.ShapeDtypeStruct((rows, width), BF16)] * Y,
        compiler_params=params(16),
        cost_estimate=pl.CostEstimate(flops=Y * rows * width, bytes_accessed=6 * Y * rows * width, transcendentals=0),
    )(kept, *received)


def add_last(own, near_parts, cross_parts):
    rows, width = near_parts[0].shape
    count = len(near_parts)

    def kernel(facts_ref, *refs):
        sums = []
        for parts in (refs[:count], refs[count : count + Y]):
            total = parts[0][...].astype(F32)
            for ref in parts[1:]:
                total += ref[...].astype(F32)
            sums.append(total)
        straight = facts_ref[S + 1] == 0
        refs[count + Y][...] = jnp.where(straight, sums[0], sums[1]).astype(BF16)
        refs[count + Y + 1][...] = jnp.where(straight, sums[1], sums[0]).astype(BF16)

    return pl.pallas_call(
        kernel,
        in_specs=[SMEM] + [VMEM] * (count + Y),
        out_specs=[VMEM] * 2,
        out_shape=[jax.ShapeDtypeStruct((rows, width), BF16)] * 2,
        compiler_params=params(16),
        cost_estimate=pl.CostEstimate(flops=8 * rows * width, bytes_accessed=16 * rows * width, transcendentals=0),
    )(own, *near_parts, *cross_parts)


def swiglu_backward(own, hidden, gate_act, up_act):
    rows, width = gate_act.shape
    half = rows // 2

    def kernel(facts_ref, first, second, gate_ref, up_ref, grad_gate_ref, grad_up_ref):
        flip = facts_ref[S] == 1
        for h, (straight, crossed) in enumerate(((first, second), (second, first))):
            here = slice(h * half, (h + 1) * half)
            value = jnp.where(flip, crossed[...].astype(F32), straight[...].astype(F32))
            gate = gate_ref[here, :].astype(F32)
            sigmoid = jax.nn.sigmoid(gate)
            grad_up_ref[here, :] = (value * gate * sigmoid).astype(BF16)
            slope = sigmoid * (1.0 + gate * (1.0 - sigmoid))
            grad_gate_ref[here, :] = (value * up_ref[here, :].astype(F32) * slope).astype(BF16)

    return pl.pallas_call(
        kernel,
        in_specs=[SMEM] + [VMEM] * 4,
        out_specs=[VMEM] * 2,
        out_shape=[jax.ShapeDtypeStruct((rows, width), BF16)] * 2,
        compiler_params=params(16),
        cost_estimate=pl.CostEstimate(flops=10 * rows * width, bytes_accessed=10 * rows * width, transcendentals=rows * width),
    )(own, *hidden, gate_act, up_act)


def on_device(grad_out, down_q, scales, gate_act, up_act):
    c = lax.axis_index("c")
    own = lax.dynamic_index_in_dim(jnp.asarray(facts()), lax.axis_index(ALL), 0, keepdims=False)

    near_own = dequantize(down_q, scales)
    cross_own = shift(near_own, "xh", XH, 1)

    rows = grad_out.shape[0] // 2
    tokens = [jnp.concatenate([grad_out, shift(grad_out, "c", C, 1)], 1)]
    around = [(i * C, (i + 1) % Z * C) for i in range(Z)] + [(i * C + 1, (i - 1) % Z * C + 1) for i in range(Z)]
    tokens[0], _ = lax.optimization_barrier((tokens[0], near_own))
    for step in range(3):
        tokens.append(lax.ppermute(tokens[-1], ("z", "c"), around))
    tokens[3], cross_own = lax.optimization_barrier((tokens[3], cross_own))
    far = lax.ppermute(lax.dynamic_slice_in_dim(tokens[3], c * rows, rows, 0), ("z", "c"), around)
    near_other = shift(near_own, "c", C, 1)
    cross_other = shift(cross_own, "c", C, 1)

    lhs, *near = product_y(own, tokens, far, near_own, near_other)
    near_y = [near[0]] + [shift(near[d], "y", Y, d) for d in range(1, Y)]
    kept, *sent = product_xl(lhs, cross_own, cross_other)
    cross = add_xl(kept, [shift(part, "xl", XL, 1) for part in sent])
    cross_parts = [cross[0]] + [shift(cross[d], "y", Y, d) for d in range(1, Y)]
    kept, sent = add_y(near_y)
    near_parts = [kept, shift(sent, "xl", XL, 1)]

    sums = add_last(own, near_parts, cross_parts)
    hidden = [lax.ppermute(sums[j], ALL, home_pairs(j)) for j in range(2)]
    return tuple(swiglu_backward(own, hidden, gate_act, up_act))


def solution(mesh):
    fine = Mesh(mesh.devices.reshape(Z, XH, XL, Y, C), ALL)
    spec = P(FSDP, TP)
    return jax.shard_map(
        on_device, mesh=fine, in_specs=(spec,) * 5, out_specs=(spec, spec), check_vma=False
    )
```

```python
import numpy as np
import jax
import jax.numpy as jnp
from jax import lax
from jax.experimental import pallas as pl
from jax.experimental.pallas import tpu as pltpu
from jax.sharding import Mesh, PartitionSpec as P

BLOCK = 128
Z, XH, XL, Y, C = 8, 2, 2, 4, 2
S = XL * Y
FSDP = ("z", "xh")
TP = ("xl", "y", "c")
ALL = FSDP + TP
BF16, F32 = jnp.bfloat16, jnp.float32
VMEM = pl.BlockSpec(memory_space=pltpu.VMEM)
SMEM = pl.BlockSpec(memory_space=pltpu.SMEM)

NUMBER = (
    ((2, 5, 6, 1, 4, 0, 3, 7), (7, 3, 2, 4, 6, 1, 5, 0)),
    ((0, 5, 4, 6, 1, 7, 2, 3), (7, 3, 1, 4, 2, 5, 6, 0)),
    ((4, 2, 7, 0, 6, 1, 5, 3), (7, 5, 1, 4, 3, 2, 0, 6)),
    ((1, 5, 6, 4, 3, 7, 2, 0), (0, 5, 2, 1, 4, 6, 3, 7)),
    ((6, 4, 1, 7, 3, 0, 5, 2), (1, 0, 7, 4, 6, 2, 5, 3)),
    ((1, 3, 2, 7, 4, 6, 0, 5), (4, 6, 7, 0, 1, 3, 2, 5)),
    ((5, 4, 2, 6, 1, 0, 3, 7), (7, 5, 2, 1, 6, 4, 3, 0)),
    ((1, 0, 2, 4, 5, 7, 6, 3), (1, 0, 6, 4, 2, 5, 3, 7)),
)


def number_of(z, s, c):
    return NUMBER[z][c][s]


def half_of(number, c):
    return c if number in (0, 7) else (number - 1) % 2


def device_index(z, xh, s, c):
    return ((z * XH + xh) * S + s) * C + c


def home_pairs(r, h):
    pairs = []
    for z in range(Z):
        for xh in range(XH):
            for s in range(S):
                for c in range(C):
                    number = number_of(z, s, c)
                    away = (number + 1) // 2
                    to = (z - away if c == 0 else z + away) % Z
                    if half_of(number, c) == h:
                        pairs.append((device_index(z, xh, s, c), device_index(to, xh, z, xh ^ r)))
    return pairs


def facts():
    rows = []
    for z in range(Z):
        for xh in range(XH):
            for xl in range(XL):
                for y in range(Y):
                    for c in range(C):
                        place = [0] * S
                        for s in range(S):
                            place[number_of(z, s, c)] = 2 * ((s % Y - y) % Y) + ((s // Y) ^ xl)
                        rows.append(place + [c, c ^ xh])
    return np.array(rows, np.int32)


def shift(x, axis, size, by):
    return lax.ppermute(x, axis, [(i, (i + by) % size) for i in range(size)])


def dequantize(values, scales):
    rows, cols = values.shape
    grid = values.astype(F32).reshape(rows // BLOCK, BLOCK, cols // BLOCK, BLOCK)
    grid = grid * scales.astype(F32)[:, None, :, None]
    return grid.reshape(rows, cols).astype(BF16)


DIMS = (((1,), (1,)), ((), ()))


def times(lhs, w_own, w_other):
    half = lhs.shape[1] // 2
    total = lax.dot_general(lhs[:, :half], w_own, DIMS, preferred_element_type=F32)
    total += lax.dot_general(lhs[:, half:], w_other, DIMS, preferred_element_type=F32)
    return total.astype(BF16)


def params(mib):
    return pltpu.CompilerParams(vmem_limit_bytes=mib * 2**20)


def product_y(own, tokens, far, w_own, w_other):
    rows, depth = far.shape
    width = w_own.shape[0]

    def kernel(facts_ref, t0, t1, t2, t3, far_ref, w_own_ref, w_other_ref, lhs_ref, *out_refs):
        lhs_ref[facts_ref[0]] = t0[pl.ds(pl.multiple_of(facts_ref[S] * rows, rows), rows), :]
        for i, ref in enumerate((t1, t2, t3)):
            for h in range(2):
                lhs_ref[facts_ref[1 + 2 * i + h]] = ref[h * rows : (h + 1) * rows, :]
        lhs_ref[facts_ref[7]] = far_ref[...]
        for d in range(Y):
            pair = lhs_ref[2 * d : 2 * d + 2].reshape(2 * rows, depth)
            total = times(pair, w_own_ref[...], w_other_ref[...])
            out_refs[d][0] = total[:rows]
            out_refs[d][1] = total[rows:]

    return pl.pallas_call(
        kernel,
        in_specs=[SMEM] + [VMEM] * 7,
        out_specs=[VMEM] * (1 + Y),
        out_shape=[jax.ShapeDtypeStruct((S, rows, depth), BF16)]
        + [jax.ShapeDtypeStruct((2, rows, width), BF16)] * Y,
        compiler_params=params(32),
        cost_estimate=pl.CostEstimate(flops=2 * S * rows * depth * width, bytes_accessed=8 * 2**20, transcendentals=0),
    )(own, *tokens, far, w_own, w_other)


def product_xl(lhs, w_own, w_other):
    _, rows, depth = lhs.shape
    width = w_own.shape[0]

    def kernel(lhs_ref, w_own_ref, w_other_ref, keep_ref, *send_refs):
        for d in range(Y):
            pair = lhs_ref[2 * d : 2 * d + 2].reshape(2 * rows, depth)
            total = times(pair, w_own_ref[...], w_other_ref[...])
            keep_ref[d] = total[:rows]
            send_refs[d // 2][d % 2] = total[rows:]

    return pl.pallas_call(
        kernel,
        in_specs=[VMEM] * 3,
        out_specs=[VMEM] * 3,
        out_shape=[jax.ShapeDtypeStruct((n, rows, width), BF16) for n in (Y, Y // 2, Y // 2)],
        compiler_params=params(32),
        cost_estimate=pl.CostEstimate(flops=2 * S * rows * depth * width, bytes_accessed=6 * 2**20, transcendentals=0),
    )(lhs, w_own, w_other)


def add_y(parts):
    _, rows, width = parts[0].shape

    def kernel(*refs):
        for e in range(2):
            total = refs[0][e].astype(F32)
            for ref in refs[1:Y]:
                total += ref[e].astype(F32)
            refs[Y + e][...] = total.astype(BF16)

    return pl.pallas_call(
        kernel,
        in_specs=[VMEM] * Y,
        out_specs=[VMEM] * 2,
        out_shape=[jax.ShapeDtypeStruct((rows, width), BF16)] * 2,
        compiler_params=params(16),
        cost_estimate=pl.CostEstimate(flops=2 * Y * rows * width, bytes_accessed=4 * (Y + 1) * rows * width, transcendentals=0),
    )(*parts)


def add_xl(kept, received):
    _, rows, width = kept.shape

    def kernel(kept_ref, low_ref, high_ref, *out_refs):
        for d in range(Y):
            received = (low_ref, high_ref)[d // 2][d % 2]
            out_refs[d][...] = (kept_ref[d].astype(F32) + received.astype(F32)).astype(BF16)

    return pl.pallas_call(
        kernel,
        in_specs=[VMEM] * 3,
        out_specs=[VMEM] * Y,
        out_shape=[jax.ShapeDtypeStruct((rows, width), BF16)] * Y,
        compiler_params=params(16),
        cost_estimate=pl.CostEstimate(flops=Y * rows * width, bytes_accessed=6 * Y * rows * width, transcendentals=0),
    )(kept, *received)


def add_last(parts):
    rows, width = parts[0].shape

    def kernel(*refs):
        total = refs[0][...].astype(F32)
        for ref in refs[1:-1]:
            total += ref[...].astype(F32)
        refs[-1][...] = total.astype(BF16)

    return pl.pallas_call(
        kernel,
        in_specs=[VMEM] * len(parts),
        out_specs=VMEM,
        out_shape=jax.ShapeDtypeStruct((rows, width), BF16),
        compiler_params=params(16),
        cost_estimate=pl.CostEstimate(flops=4 * rows * width, bytes_accessed=8 * rows * width, transcendentals=0),
    )(*parts)


def swiglu_backward(own, hidden, gate_act, up_act):
    rows, width = gate_act.shape
    half = rows // 2

    def kernel(facts_ref, near0, near1, cross0, cross1, gate_ref, up_ref, grad_gate_ref, grad_up_ref):
        crossed = facts_ref[S + 1] == 1
        for h, (near, cross) in enumerate(((near0, cross0), (near1, cross1))):
            here = slice(h * half, (h + 1) * half)
            value = jnp.where(crossed, cross[...].astype(F32), near[...].astype(F32))
            gate = gate_ref[here, :].astype(F32)
            sigmoid = jax.nn.sigmoid(gate)
            grad_up_ref[here, :] = (value * gate * sigmoid).astype(BF16)
            slope = sigmoid * (1.0 + gate * (1.0 - sigmoid))
            grad_gate_ref[here, :] = (value * up_ref[here, :].astype(F32) * slope).astype(BF16)

    return pl.pallas_call(
        kernel,
        in_specs=[SMEM] + [VMEM] * 6,
        out_specs=[VMEM] * 2,
        out_shape=[jax.ShapeDtypeStruct((rows, width), BF16)] * 2,
        compiler_params=params(16),
        cost_estimate=pl.CostEstimate(flops=10 * rows * width, bytes_accessed=10 * rows * width, transcendentals=rows * width),
    )(own, *hidden[0], *hidden[1], gate_act, up_act)


def on_device(grad_out, down_q, scales, gate_act, up_act):
    c = lax.axis_index("c")
    own = lax.dynamic_index_in_dim(jnp.asarray(facts()), lax.axis_index(ALL), 0, keepdims=False)

    near_own = dequantize(down_q, scales)
    cut = 5 * BLOCK
    cross_parts = [shift(near_own[:cut], "xh", XH, 1), shift(near_own[cut:], "xh", XH, 1)]

    rows = grad_out.shape[0] // 2
    tokens = [jnp.concatenate([grad_out, shift(grad_out, "c", C, 1)], 1)]
    around = [(i * C, (i + 1) % Z * C) for i in range(Z)] + [(i * C + 1, (i - 1) % Z * C + 1) for i in range(Z)]
    tokens[0], _ = lax.optimization_barrier((tokens[0], near_own))
    for step in range(3):
        if step == 2:
            tokens[-1], cross_parts[0] = lax.optimization_barrier((tokens[-1], cross_parts[0]))
        tokens.append(lax.ppermute(tokens[-1], ("z", "c"), around))
    tokens[3], cross_parts[1] = lax.optimization_barrier((tokens[3], cross_parts[1]))
    far = lax.ppermute(lax.dynamic_slice_in_dim(tokens[3], c * rows, rows, 0), ("z", "c"), around)
    near_other = shift(near_own, "c", C, 1)
    cross_own = jnp.concatenate(cross_parts, 0)
    cross_other = shift(cross_own, "c", C, 1)

    lhs, *near = product_y(own, tokens, far, near_own, near_other)
    near_y = [near[0]] + [shift(near[d], "y", Y, d) for d in range(1, Y)]
    kept, *sent = product_xl(lhs, cross_own, cross_other)
    cross = add_xl(kept, [shift(part, "xl", XL, 1) for part in sent])
    cross_parts = [cross[0]] + [shift(cross[d], "y", Y, d) for d in range(1, Y)]
    kept, sent = add_y(near_y)
    near_parts = [kept, shift(sent, "xl", XL, 1)]

    sums = [add_last(near_parts), add_last(cross_parts)]
    hidden = [[lax.ppermute(sums[r], ALL, home_pairs(r, h)) for h in range(2)] for r in range(2)]
    return tuple(swiglu_backward(own, hidden, gate_act, up_act))


def solution(mesh):
    fine = Mesh(mesh.devices.reshape(Z, XH, XL, Y, C), ALL)
    spec = P(FSDP, TP)
    return jax.shard_map(
        on_device, mesh=fine, in_specs=(spec,) * 5, out_specs=(spec, spec), check_vma=False
    )
```

```python
import numpy as np
import jax
import jax.numpy as jnp
from jax import lax
from jax.experimental import pallas as pl
from jax.experimental.pallas import tpu as pltpu
from jax.sharding import Mesh, PartitionSpec as P

BLOCK = 128
Z, XH, XL, Y, C = 8, 2, 2, 4, 2
S = XL * Y
FSDP = ("z", "xh")
TP = ("xl", "y", "c")
ALL = FSDP + TP
BF16, F32 = jnp.bfloat16, jnp.float32
VMEM = pl.BlockSpec(memory_space=pltpu.VMEM)
SMEM = pl.BlockSpec(memory_space=pltpu.SMEM)

NUMBER = (
    ((2, 5, 6, 1, 4, 0, 3, 7), (7, 3, 2, 4, 6, 1, 5, 0)),
    ((0, 5, 4, 6, 1, 7, 2, 3), (7, 3, 1, 4, 2, 5, 6, 0)),
    ((4, 2, 7, 0, 6, 1, 5, 3), (7, 5, 1, 4, 3, 2, 0, 6)),
    ((1, 5, 6, 4, 3, 7, 2, 0), (0, 5, 2, 1, 4, 6, 3, 7)),
    ((6, 4, 1, 7, 3, 0, 5, 2), (1, 0, 7, 4, 6, 2, 5, 3)),
    ((1, 3, 2, 7, 4, 6, 0, 5), (4, 6, 7, 0, 1, 3, 2, 5)),
    ((5, 4, 2, 6, 1, 0, 3, 7), (7, 5, 2, 1, 6, 4, 3, 0)),
    ((1, 0, 2, 4, 5, 7, 6, 3), (1, 0, 6, 4, 2, 5, 3, 7)),
)


def number_of(z, s, c):
    return NUMBER[z][c][s]


def half_of(number, c):
    return c if number in (0, 7) else (number - 1) % 2


def device_index(z, xh, s, c):
    return ((z * XH + xh) * S + s) * C + c


def home_pairs(r, h):
    pairs = []
    for z in range(Z):
        for xh in range(XH):
            for s in range(S):
                for c in range(C):
                    number = number_of(z, s, c)
                    away = (number + 1) // 2
                    to = (z - away if c == 0 else z + away) % Z
                    if half_of(number, c) == h:
                        pairs.append((device_index(z, xh, s, c), device_index(to, xh, z, xh ^ r)))
    return pairs


def facts():
    rows = []
    for z in range(Z):
        for xh in range(XH):
            for xl in range(XL):
                for y in range(Y):
                    for c in range(C):
                        place = [0] * S
                        for s in range(S):
                            place[number_of(z, s, c)] = ((s // Y) ^ xl) * Y + (s % Y - y) % Y
                        rows.append(place + [c, c ^ xh])
    return np.array(rows, np.int32)


def shift(x, axis, size, by):
    return lax.ppermute(x, axis, [(i, (i + by) % size) for i in range(size)])


def dequantize(values, scales):
    rows, cols = values.shape
    grid = values.astype(F32).reshape(rows // BLOCK, BLOCK, cols // BLOCK, BLOCK)
    grid = grid * scales.astype(F32)[:, None, :, None]
    return grid.reshape(rows, cols).astype(BF16)


DIMS = (((1,), (1,)), ((), ()))


def times(lhs, w_own, w_other):
    half = lhs.shape[1] // 2
    total = lax.dot_general(lhs[:, :half], w_own, DIMS, preferred_element_type=F32)
    total += lax.dot_general(lhs[:, half:], w_other, DIMS, preferred_element_type=F32)
    return total.astype(BF16)


def params(mib):
    return pltpu.CompilerParams(vmem_limit_bytes=mib * 2**20)


def product_send(own, tokens, far, w_own, w_other):
    rows, depth = far.shape
    width = w_own.shape[0]

    def kernel(facts_ref, t0, t1, t2, t3, far_ref, w_own_ref, w_other_ref, lhs_ref, *send_refs):
        lhs_ref[facts_ref[0]] = t0[pl.ds(pl.multiple_of(facts_ref[S] * rows, rows), rows), :]
        for i, ref in enumerate((t1, t2, t3)):
            for h in range(2):
                lhs_ref[facts_ref[1 + 2 * i + h]] = ref[h * rows : (h + 1) * rows, :]
        lhs_ref[facts_ref[7]] = far_ref[...]
        for i in range(2):
            total = times(lhs_ref[Y + 2 * i : Y + 2 * i + 2].reshape(2 * rows, depth), w_own_ref[...], w_other_ref[...])
            send_refs[i][0] = total[:rows]
            send_refs[i][1] = total[rows:]

    return pl.pallas_call(
        kernel,
        in_specs=[SMEM] + [VMEM] * 7,
        out_specs=[VMEM] * 3,
        out_shape=[jax.ShapeDtypeStruct((S, rows, depth), BF16)]
        + [jax.ShapeDtypeStruct((2, rows, width), BF16)] * 2,
        compiler_params=params(32),
        cost_estimate=pl.CostEstimate(flops=S * rows * depth * width, bytes_accessed=7 * 2**20, transcendentals=0),
    )(own, *tokens, far, w_own, w_other)


def product_y(lhs, w_own, w_other):
    _, rows, depth = lhs.shape
    width = w_own.shape[0]

    def kernel(lhs_ref, w_own_ref, w_other_ref, *out_refs):
        for e in range(2):
            total = times(lhs_ref[Y * e : Y * e + Y].reshape(Y * rows, depth), w_own_ref[...], w_other_ref[...])
            for d in range(Y):
                out_refs[d][e] = total[d * rows : (d + 1) * rows]

    return pl.pallas_call(
        kernel,
        in_specs=[VMEM] * 3,
        out_specs=[VMEM] * Y,
        out_shape=[jax.ShapeDtypeStruct((2, rows, width), BF16)] * Y,
        compiler_params=params(32),
        cost_estimate=pl.CostEstimate(flops=2 * S * rows * depth * width, bytes_accessed=6 * 2**20, transcendentals=0),
    )(lhs, w_own, w_other)


def product_keep(lhs, w_own, w_other):
    _, rows, depth = lhs.shape
    width = w_own.shape[0]

    def kernel(lhs_ref, w_own_ref, w_other_ref, keep_ref):
        total = times(lhs_ref[...].reshape(Y * rows, depth), w_own_ref[...], w_other_ref[...])
        for d in range(Y):
            keep_ref[d] = total[d * rows : (d + 1) * rows]

    return pl.pallas_call(
        kernel,
        grid=(1,),
        in_specs=[
            pl.BlockSpec((Y, rows, depth), lambda i: (0, 0, 0)),
            pl.BlockSpec(w_own.shape, lambda i: (0, 0)),
            pl.BlockSpec(w_own.shape, lambda i: (0, 0)),
        ],
        out_specs=pl.BlockSpec((Y, rows, width), lambda i: (0, 0, 0)),
        out_shape=jax.ShapeDtypeStruct((Y, rows, width), BF16),
        compiler_params=params(32),
        cost_estimate=pl.CostEstimate(flops=S * rows * depth * width, bytes_accessed=4 * 2**20, transcendentals=0),
    )(lhs, w_own, w_other)


def add_y(parts):
    _, rows, width = parts[0].shape

    def kernel(*refs):
        for e in range(2):
            total = refs[0][e].astype(F32)
            for ref in refs[1:Y]:
                total += ref[e].astype(F32)
            refs[Y + e][...] = total.astype(BF16)

    return pl.pallas_call(
        kernel,
        in_specs=[VMEM] * Y,
        out_specs=[VMEM] * 2,
        out_shape=[jax.ShapeDtypeStruct((rows, width), BF16)] * 2,
        compiler_params=params(16),
        cost_estimate=pl.CostEstimate(flops=2 * Y * rows * width, bytes_accessed=4 * (Y + 1) * rows * width, transcendentals=0),
    )(*parts)


def add_xl(kept, received):
    _, rows, width = kept.shape

    def kernel(kept_ref, low_ref, high_ref, *out_refs):
        for d in range(Y):
            received = (low_ref, high_ref)[d // 2][d % 2]
            out_refs[d][...] = (kept_ref[d].astype(F32) + received.astype(F32)).astype(BF16)

    return pl.pallas_call(
        kernel,
        in_specs=[VMEM] * 3,
        out_specs=[VMEM] * Y,
        out_shape=[jax.ShapeDtypeStruct((rows, width), BF16)] * Y,
        compiler_params=params(16),
        cost_estimate=pl.CostEstimate(flops=Y * rows * width, bytes_accessed=6 * Y * rows * width, transcendentals=0),
    )(kept, *received)


def add_last(parts):
    rows, width = parts[0].shape

    def kernel(*refs):
        total = refs[0][...].astype(F32)
        for ref in refs[1:-1]:
            total += ref[...].astype(F32)
        refs[-1][...] = total.astype(BF16)

    return pl.pallas_call(
        kernel,
        in_specs=[VMEM] * len(parts),
        out_specs=VMEM,
        out_shape=jax.ShapeDtypeStruct((rows, width), BF16),
        compiler_params=params(16),
        cost_estimate=pl.CostEstimate(flops=4 * rows * width, bytes_accessed=8 * rows * width, transcendentals=0),
    )(*parts)


def swiglu_backward(own, hidden, gate_act, up_act):
    rows, width = gate_act.shape
    half = rows // 2

    def kernel(facts_ref, near0, near1, cross0, cross1, gate_ref, up_ref, grad_gate_ref, grad_up_ref):
        crossed = facts_ref[S + 1] == 1
        for h, (near, cross) in enumerate(((near0, cross0), (near1, cross1))):
            here = slice(h * half, (h + 1) * half)
            value = jnp.where(crossed, cross[...].astype(F32), near[...].astype(F32))
            gate = gate_ref[here, :].astype(F32)
            sigmoid = jax.nn.sigmoid(gate)
            grad_up_ref[here, :] = (value * gate * sigmoid).astype(BF16)
            slope = sigmoid * (1.0 + gate * (1.0 - sigmoid))
            grad_gate_ref[here, :] = (value * up_ref[here, :].astype(F32) * slope).astype(BF16)

    return pl.pallas_call(
        kernel,
        in_specs=[SMEM] + [VMEM] * 6,
        out_specs=[VMEM] * 2,
        out_shape=[jax.ShapeDtypeStruct((rows, width), BF16)] * 2,
        compiler_params=params(16),
        cost_estimate=pl.CostEstimate(flops=10 * rows * width, bytes_accessed=10 * rows * width, transcendentals=rows * width),
    )(own, *hidden[0], *hidden[1], gate_act, up_act)


def on_device(grad_out, down_q, scales, gate_act, up_act):
    c = lax.axis_index("c")
    own = lax.dynamic_index_in_dim(jnp.asarray(facts()), lax.axis_index(ALL), 0, keepdims=False)

    near_own = dequantize(down_q, scales)
    cut = 5 * BLOCK
    cross_parts = [shift(near_own[:cut], "xh", XH, 1), shift(near_own[cut:], "xh", XH, 1)]

    rows = grad_out.shape[0] // 2
    tokens = [jnp.concatenate([grad_out, shift(grad_out, "c", C, 1)], 1)]
    around = [(i * C, (i + 1) % Z * C) for i in range(Z)] + [(i * C + 1, (i - 1) % Z * C + 1) for i in range(Z)]
    tokens[0], _ = lax.optimization_barrier((tokens[0], near_own))
    for step in range(3):
        if step == 2:
            tokens[-1], cross_parts[0] = lax.optimization_barrier((tokens[-1], cross_parts[0]))
        tokens.append(lax.ppermute(tokens[-1], ("z", "c"), around))
    tokens[3], cross_parts[1] = lax.optimization_barrier((tokens[3], cross_parts[1]))
    far = lax.ppermute(lax.dynamic_slice_in_dim(tokens[3], c * rows, rows, 0), ("z", "c"), around)
    near_other = shift(near_own, "c", C, 1)
    cross_own = jnp.concatenate(cross_parts, 0)
    cross_other = shift(cross_own, "c", C, 1)

    lhs, *sent = product_send(own, tokens, far, cross_own, cross_other)
    near = product_y(lhs, near_own, near_other)
    near_y = [near[0]] + [shift(near[d], "y", Y, d) for d in range(1, Y)]
    kept = product_keep(lhs, cross_own, cross_other)
    cross = add_xl(kept, [shift(part, "xl", XL, 1) for part in sent])
    cross_parts = [cross[0]] + [shift(cross[d], "y", Y, d) for d in range(1, Y)]
    kept, sent = add_y(near_y)
    near_parts = [kept, shift(sent, "xl", XL, 1)]

    sums = [add_last(near_parts), add_last(cross_parts)]
    hidden = [[lax.ppermute(sums[r], ALL, home_pairs(r, h)) for h in range(2)] for r in range(2)]
    return tuple(swiglu_backward(own, hidden, gate_act, up_act))


def solution(mesh):
    fine = Mesh(mesh.devices.reshape(Z, XH, XL, Y, C), ALL)
    spec = P(FSDP, TP)
    return jax.shard_map(
        on_device, mesh=fine, in_specs=(spec,) * 5, out_specs=(spec, spec), check_vma=False
    )
```

```python
import numpy as np
import jax
import jax.numpy as jnp
from jax import lax
from jax.experimental import pallas as pl
from jax.experimental.pallas import tpu as pltpu
from jax.sharding import Mesh, PartitionSpec as P

BLOCK = 128
Z, XH, XL, Y, C = 8, 2, 2, 4, 2
S = XL * Y
FSDP = ("z", "xh")
TP = ("xl", "y", "c")
ALL = FSDP + TP
BF16, F32 = jnp.bfloat16, jnp.float32
VMEM = pl.BlockSpec(memory_space=pltpu.VMEM)
SMEM = pl.BlockSpec(memory_space=pltpu.SMEM)
HBM = pl.BlockSpec(memory_space=pltpu.MemorySpace.HBM)

NUMBER = (
    ((2, 5, 6, 1, 4, 0, 3, 7), (7, 3, 2, 4, 6, 1, 5, 0)),
    ((0, 5, 4, 6, 1, 7, 2, 3), (7, 3, 1, 4, 2, 5, 6, 0)),
    ((4, 2, 7, 0, 6, 1, 5, 3), (7, 5, 1, 4, 3, 2, 0, 6)),
    ((1, 5, 6, 4, 3, 7, 2, 0), (0, 5, 2, 1, 4, 6, 3, 7)),
    ((6, 4, 1, 7, 3, 0, 5, 2), (1, 0, 7, 4, 6, 2, 5, 3)),
    ((1, 3, 2, 7, 4, 6, 0, 5), (4, 6, 7, 0, 1, 3, 2, 5)),
    ((5, 4, 2, 6, 1, 0, 3, 7), (7, 5, 2, 1, 6, 4, 3, 0)),
    ((1, 0, 2, 4, 5, 7, 6, 3), (1, 0, 6, 4, 2, 5, 3, 7)),
)


def number_of(z, s, c):
    return NUMBER[z][c][s]


def half_of(number, c):
    return c if number in (0, 7) else (number - 1) % 2


def device_index(z, xh, s, c):
    return ((z * XH + xh) * S + s) * C + c


def home_pairs(j):
    pairs = []
    for z in range(Z):
        for xh in range(XH):
            for s in range(S):
                for c in range(C):
                    number = number_of(z, s, c)
                    away = (number + 1) // 2
                    to = (z - away if c == 0 else z + away) % Z
                    pairs.append((device_index(z, xh, s, c), device_index(to, xh, z, j ^ half_of(number, c))))
    return pairs


def facts():
    rows = []
    for z in range(Z):
        for xh in range(XH):
            for xl in range(XL):
                for y in range(Y):
                    for c in range(C):
                        place = [0] * S
                        for s in range(S):
                            place[number_of(z, s, c)] = ((s // Y) ^ xl) * Y + (s % Y - y) % Y
                        rows.append(place + [c, half_of(number_of(z, xl * Y + y, c), c) ^ xh])
    return np.array(rows, np.int32)


def shift(x, axis, size, by):
    return lax.ppermute(x, axis, [(i, (i + by) % size) for i in range(size)])


def dequantize(values, scales):
    rows, cols = values.shape
    grid = values.astype(F32).reshape(rows // BLOCK, BLOCK, cols // BLOCK, BLOCK)
    grid = grid * scales.astype(F32)[:, None, :, None]
    return grid.reshape(rows, cols).astype(BF16)


DIMS = (((1,), (1,)), ((), ()))


def times(lhs, w_own, w_other):
    half = lhs.shape[1] // 2
    total = lax.dot_general(lhs[:, :half], w_own, DIMS, preferred_element_type=F32)
    total += lax.dot_general(lhs[:, half:], w_other, DIMS, preferred_element_type=F32)
    return total.astype(BF16)


def params(mib):
    return pltpu.CompilerParams(vmem_limit_bytes=mib * 2**20)


def product_y(own, tokens, far, w_own, w_other):
    rows, depth = far.shape
    width = w_own.shape[0]

    def kernel(facts_ref, t0, t1, t2, t3, far_ref, w_own_ref, w_other_ref, lhs_ref, *refs):
        out_refs, sems = refs[:Y], refs[Y]
        blocks = [t0.at[pl.ds(pl.multiple_of(facts_ref[S] * rows, rows), rows), :]]
        blocks += [ref.at[h * rows : (h + 1) * rows, :] for ref in (t1, t2, t3) for h in range(2)] + [far_ref]
        copies = [pltpu.make_async_copy(block, lhs_ref.at[facts_ref[i]], sems.at[i]) for i, block in enumerate(blocks)]
        for copy in copies:
            copy.start()
        for copy in copies:
            copy.wait()
        for e in range(2):
            total = times(lhs_ref[Y * e : Y * e + Y].reshape(Y * rows, depth), w_own_ref[...], w_other_ref[...])
            for d in range(Y):
                out_refs[d][e] = total[d * rows : (d + 1) * rows]

    return pl.pallas_call(
        kernel,
        in_specs=[SMEM] + [HBM] * 5 + [VMEM] * 2,
        out_specs=[VMEM] * (1 + Y),
        out_shape=[jax.ShapeDtypeStruct((S, rows, depth), BF16)]
        + [jax.ShapeDtypeStruct((2, rows, width), BF16)] * Y,
        scratch_shapes=[pltpu.SemaphoreType.DMA((S,))],
        compiler_params=params(56),
        cost_estimate=pl.CostEstimate(flops=2 * S * rows * depth * width, bytes_accessed=8 * 2**20, transcendentals=0),
    )(own, *tokens, far, w_own, w_other)


def product_xl(lhs, w_own, w_other, e):
    _, rows, depth = lhs.shape
    width = w_own.shape[0]

    def kernel(lhs_ref, w_own_ref, w_other_ref, *out_refs):
        total = times(lhs_ref[...].reshape(Y * rows, depth), w_own_ref[...], w_other_ref[...])
        for d in range(Y):
            out_refs[d // 2][d % 2] = total[d * rows : (d + 1) * rows]

    whole = lambda *shape: pl.BlockSpec(shape, lambda i: (0,) * len(shape))
    return pl.pallas_call(
        kernel,
        grid=(1,),
        in_specs=[pl.BlockSpec((Y, rows, depth), lambda i: (e, 0, 0)), whole(width, depth // 2), whole(width, depth // 2)],
        out_specs=[whole(2, rows, width)] * 2,
        out_shape=[jax.ShapeDtypeStruct((2, rows, width), BF16)] * 2,
        compiler_params=params(16),
        cost_estimate=pl.CostEstimate(flops=S * rows * depth * width, bytes_accessed=4 * 2**20, transcendentals=0),
    )(lhs, w_own, w_other)


def add_y(parts):
    _, rows, width = parts[0].shape

    def kernel(*refs):
        for e in range(2):
            total = refs[0][e].astype(F32)
            for ref in refs[1:Y]:
                total += ref[e].astype(F32)
            refs[Y + e][...] = total.astype(BF16)

    return pl.pallas_call(
        kernel,
        in_specs=[VMEM] * Y,
        out_specs=[VMEM] * 2,
        out_shape=[jax.ShapeDtypeStruct((rows, width), BF16)] * 2,
        compiler_params=params(16),
        cost_estimate=pl.CostEstimate(flops=2 * Y * rows * width, bytes_accessed=4 * (Y + 1) * rows * width, transcendentals=0),
    )(*parts)


def add_xl(kept, received):
    _, rows, width = kept[0].shape

    def kernel(*refs):
        kept_refs, received_refs, out_refs = refs[:2], refs[2:4], refs[4:]
        for d in range(Y):
            total = kept_refs[d // 2][d % 2].astype(F32) + received_refs[d // 2][d % 2].astype(F32)
            out_refs[d][...] = total.astype(BF16)

    return pl.pallas_call(
        kernel,
        in_specs=[VMEM] * 4,
        out_specs=[VMEM] * Y,
        out_shape=[jax.ShapeDtypeStruct((rows, width), BF16)] * Y,
        compiler_params=params(16),
        cost_estimate=pl.CostEstimate(flops=Y * rows * width, bytes_accessed=6 * Y * rows * width, transcendentals=0),
    )(*kept, *received)


def add_last(own, near_parts, cross_parts):
    rows, width = near_parts[0].shape
    count = len(near_parts)

    def kernel(facts_ref, *refs):
        sums = []
        for parts in (refs[:count], refs[count : count + Y]):
            total = parts[0][...].astype(F32)
            for ref in parts[1:]:
                total += ref[...].astype(F32)
            sums.append(total)
        straight = facts_ref[S + 1] == 0
        refs[count + Y][...] = jnp.where(straight, sums[0], sums[1]).astype(BF16)
        refs[count + Y + 1][...] = jnp.where(straight, sums[1], sums[0]).astype(BF16)

    return pl.pallas_call(
        kernel,
        in_specs=[SMEM] + [VMEM] * (count + Y),
        out_specs=[VMEM] * 2,
        out_shape=[jax.ShapeDtypeStruct((rows, width), BF16)] * 2,
        compiler_params=params(16),
        cost_estimate=pl.CostEstimate(flops=8 * rows * width, bytes_accessed=16 * rows * width, transcendentals=0),
    )(own, *near_parts, *cross_parts)


def swiglu_backward(own, hidden, gate_act, up_act):
    rows, width = gate_act.shape
    half = rows // 2

    def kernel(facts_ref, first, second, gate_ref, up_ref, grad_gate_ref, grad_up_ref):
        flip = facts_ref[S] == 1
        for h, (straight, crossed) in enumerate(((first, second), (second, first))):
            here = slice(h * half, (h + 1) * half)
            value = jnp.where(flip, crossed[...].astype(F32), straight[...].astype(F32))
            gate = gate_ref[here, :].astype(F32)
            sigmoid = jax.nn.sigmoid(gate)
            grad_up_ref[here, :] = (value * gate * sigmoid).astype(BF16)
            slope = sigmoid * (1.0 + gate * (1.0 - sigmoid))
            grad_gate_ref[here, :] = (value * up_ref[here, :].astype(F32) * slope).astype(BF16)

    return pl.pallas_call(
        kernel,
        in_specs=[SMEM] + [VMEM] * 4,
        out_specs=[VMEM] * 2,
        out_shape=[jax.ShapeDtypeStruct((rows, width), BF16)] * 2,
        compiler_params=params(16),
        cost_estimate=pl.CostEstimate(flops=10 * rows * width, bytes_accessed=10 * rows * width, transcendentals=rows * width),
    )(own, *hidden, gate_act, up_act)


def on_device(grad_out, down_q, scales, gate_act, up_act):
    c = lax.axis_index("c")
    own = lax.dynamic_index_in_dim(jnp.asarray(facts()), lax.axis_index(ALL), 0, keepdims=False)

    near_own = dequantize(down_q, scales)
    near_other = shift(near_own, "c", C, 1)
    cut = 5 * BLOCK
    cross_own = [shift(near_own[:cut], "xh", XH, 1), shift(near_own[cut:], "xh", XH, 1)]

    rows = grad_out.shape[0] // 2
    tokens = [jnp.concatenate([grad_out, shift(grad_out, "c", C, 1)], 1)]
    around = [(i * C, (i + 1) % Z * C) for i in range(Z)] + [(i * C + 1, (i - 1) % Z * C + 1) for i in range(Z)]
    tokens[0], _ = lax.optimization_barrier((tokens[0], near_own))
    for step in range(3):
        if step == 2:
            tokens[2], cross_own[0], near_other = lax.optimization_barrier((tokens[2], cross_own[0], near_other))
        tokens.append(lax.ppermute(tokens[-1], ("z", "c"), around))
    tokens[3], cross_own[1] = lax.optimization_barrier((tokens[3], cross_own[1]))
    far = lax.ppermute(lax.dynamic_slice_in_dim(tokens[3], c * rows, rows, 0), ("z", "c"), around)
    cross_own, far = lax.optimization_barrier((jnp.concatenate(cross_own, 0), far))
    cross_other = shift(cross_own, "c", C, 1)

    lhs, *near = product_y(own, tokens, far, near_own, near_other)
    near_y = [near[0]] + [shift(near[d], "y", Y, d) for d in range(1, Y)]
    sent = product_xl(lhs, cross_own, cross_other, 1)
    kept = product_xl(lhs, cross_own, cross_other, 0)
    cross = add_xl(kept, [shift(part, "xl", XL, 1) for part in sent])
    cross_parts = [cross[0]] + [shift(cross[d], "y", Y, d) for d in range(1, Y)]
    kept, sent = add_y(near_y)
    near_parts = [kept, shift(sent, "xl", XL, 1)]

    sums = add_last(own, near_parts, cross_parts)
    hidden = [lax.ppermute(sums[j], ALL, home_pairs(j)) for j in range(2)]
    return tuple(swiglu_backward(own, hidden, gate_act, up_act))


def solution(mesh):
    fine = Mesh(mesh.devices.reshape(Z, XH, XL, Y, C), ALL)
    spec = P(FSDP, TP)
    return jax.shard_map(
        on_device, mesh=fine, in_specs=(spec,) * 5, out_specs=(spec, spec), check_vma=False
    )
```

```python
import numpy as np
import jax
import jax.numpy as jnp
from jax import lax
from jax.experimental import pallas as pl
from jax.experimental.pallas import tpu as pltpu
from jax.sharding import Mesh, PartitionSpec as P

BLOCK = 128
Z, XH, XL, Y, C = 8, 2, 2, 4, 2
S = XL * Y
FSDP = ("z", "xh")
TP = ("xl", "y", "c")
ALL = FSDP + TP
BF16, F32 = jnp.bfloat16, jnp.float32
VMEM = pl.BlockSpec(memory_space=pltpu.VMEM)
SMEM = pl.BlockSpec(memory_space=pltpu.SMEM)

NUMBER = (
    ((2, 5, 6, 1, 4, 0, 3, 7), (7, 3, 2, 4, 6, 1, 5, 0)),
    ((0, 5, 4, 6, 1, 7, 2, 3), (7, 3, 1, 4, 2, 5, 6, 0)),
    ((4, 2, 7, 0, 6, 1, 5, 3), (7, 5, 1, 4, 3, 2, 0, 6)),
    ((1, 5, 6, 4, 3, 7, 2, 0), (0, 5, 2, 1, 4, 6, 3, 7)),
    ((6, 4, 1, 7, 3, 0, 5, 2), (1, 0, 7, 4, 6, 2, 5, 3)),
    ((1, 3, 2, 7, 4, 6, 0, 5), (4, 6, 7, 0, 1, 3, 2, 5)),
    ((5, 4, 2, 6, 1, 0, 3, 7), (7, 5, 2, 1, 6, 4, 3, 0)),
    ((1, 0, 2, 4, 5, 7, 6, 3), (1, 0, 6, 4, 2, 5, 3, 7)),
)


def number_of(z, s, c):
    return NUMBER[z][c][s]


def half_of(number, c):
    return c if number in (0, 7) else (number - 1) % 2


def device_index(z, xh, s, c):
    return ((z * XH + xh) * S + s) * C + c


def home_pairs(r, h):
    pairs = []
    for z in range(Z):
        for xh in range(XH):
            for s in range(S):
                for c in range(C):
                    number = number_of(z, s, c)
                    away = (number + 1) // 2
                    to = (z - away if c == 0 else z + away) % Z
                    if half_of(number, c) == h:
                        pairs.append((device_index(z, xh, s, c), device_index(to, xh, z, xh ^ r)))
    return pairs


def facts():
    rows = []
    for z in range(Z):
        for xh in range(XH):
            for xl in range(XL):
                for y in range(Y):
                    for c in range(C):
                        place = [0] * S
                        for s in range(S):
                            place[number_of(z, s, c)] = ((s // Y) ^ xl) * Y + (s % Y - y) % Y
                        rows.append(place + [c, c ^ xh])
    return np.array(rows, np.int32)


def shift(x, axis, size, by):
    return lax.ppermute(x, axis, [(i, (i + by) % size) for i in range(size)])


def dequantize(values, scales):
    rows, cols = values.shape
    grid = values.astype(F32).reshape(rows // BLOCK, BLOCK, cols // BLOCK, BLOCK)
    grid = grid * scales.astype(F32)[:, None, :, None]
    return grid.reshape(rows, cols).astype(BF16)


DIMS = (((1,), (1,)), ((), ()))


def times(lhs, w_own, w_other):
    half = lhs.shape[1] // 2
    total = lax.dot_general(lhs[:, :half], w_own, DIMS, preferred_element_type=F32)
    total += lax.dot_general(lhs[:, half:], w_other, DIMS, preferred_element_type=F32)
    return total.astype(BF16)


def params(mib):
    return pltpu.CompilerParams(vmem_limit_bytes=mib * 2**20)


def product_y(own, tokens, far, w_own, w_other):
    rows, depth = far.shape
    width = w_own.shape[0]

    def kernel(facts_ref, t0, t1, t2, t3, far_ref, w_own_ref, w_other_ref, lhs_ref, *out_refs):
        lhs_ref[facts_ref[0]] = t0[pl.ds(pl.multiple_of(facts_ref[S] * rows, rows), rows), :]
        for i, ref in enumerate((t1, t2, t3)):
            for h in range(2):
                lhs_ref[facts_ref[1 + 2 * i + h]] = ref[h * rows : (h + 1) * rows, :]
        lhs_ref[facts_ref[7]] = far_ref[...]
        for e in range(2):
            total = times(lhs_ref[Y * e : Y * e + Y].reshape(Y * rows, depth), w_own_ref[...], w_other_ref[...])
            for d in range(Y):
                out_refs[d][e] = total[d * rows : (d + 1) * rows]

    return pl.pallas_call(
        kernel,
        in_specs=[SMEM] + [VMEM] * 7,
        out_specs=[VMEM] * (1 + Y),
        out_shape=[jax.ShapeDtypeStruct((S, rows, depth), BF16)]
        + [jax.ShapeDtypeStruct((2, rows, width), BF16)] * Y,
        compiler_params=params(32),
        cost_estimate=pl.CostEstimate(flops=2 * S * rows * depth * width, bytes_accessed=8 * 2**20, transcendentals=0),
    )(own, *tokens, far, w_own, w_other)


def product_xl(lhs, w_own, w_other, e):
    _, rows, depth = lhs.shape
    width = w_own.shape[0]

    def kernel(lhs_ref, w_own_ref, w_other_ref, *out_refs):
        total = times(lhs_ref[...].reshape(Y * rows, depth), w_own_ref[...], w_other_ref[...])
        for d in range(Y):
            out_refs[d // 2][d % 2] = total[d * rows : (d + 1) * rows]

    whole = lambda *shape: pl.BlockSpec(shape, lambda i: (0,) * len(shape))
    return pl.pallas_call(
        kernel,
        grid=(1,),
        in_specs=[pl.BlockSpec((Y, rows, depth), lambda i: (e, 0, 0)), whole(width, depth // 2), whole(width, depth // 2)],
        out_specs=[whole(2, rows, width)] * 2,
        out_shape=[jax.ShapeDtypeStruct((2, rows, width), BF16)] * 2,
        compiler_params=params(16),
        cost_estimate=pl.CostEstimate(flops=S * rows * depth * width, bytes_accessed=4 * 2**20, transcendentals=0),
    )(lhs, w_own, w_other)


def add_y(parts):
    _, rows, width = parts[0].shape

    def kernel(*refs):
        for e in range(2):
            total = refs[0][e].astype(F32)
            for ref in refs[1:Y]:
                total += ref[e].astype(F32)
            refs[Y + e][...] = total.astype(BF16)

    return pl.pallas_call(
        kernel,
        in_specs=[VMEM] * Y,
        out_specs=[VMEM] * 2,
        out_shape=[jax.ShapeDtypeStruct((rows, width), BF16)] * 2,
        compiler_params=params(16),
        cost_estimate=pl.CostEstimate(flops=2 * Y * rows * width, bytes_accessed=4 * (Y + 1) * rows * width, transcendentals=0),
    )(*parts)


def add_xl(kept, received):
    _, rows, width = kept[0].shape

    def kernel(*refs):
        kept_refs, received_refs, out_refs = refs[:2], refs[2:4], refs[4:]
        for d in range(Y):
            total = kept_refs[d // 2][d % 2].astype(F32) + received_refs[d // 2][d % 2].astype(F32)
            out_refs[d][...] = total.astype(BF16)

    return pl.pallas_call(
        kernel,
        in_specs=[VMEM] * 4,
        out_specs=[VMEM] * Y,
        out_shape=[jax.ShapeDtypeStruct((rows, width), BF16)] * Y,
        compiler_params=params(16),
        cost_estimate=pl.CostEstimate(flops=Y * rows * width, bytes_accessed=6 * Y * rows * width, transcendentals=0),
    )(*kept, *received)


def add_last(parts):
    rows, width = parts[0].shape

    def kernel(*refs):
        total = refs[0][...].astype(F32)
        for ref in refs[1:-1]:
            total += ref[...].astype(F32)
        refs[-1][...] = total.astype(BF16)

    return pl.pallas_call(
        kernel,
        in_specs=[VMEM] * len(parts),
        out_specs=VMEM,
        out_shape=jax.ShapeDtypeStruct((rows, width), BF16),
        compiler_params=params(16),
        cost_estimate=pl.CostEstimate(flops=4 * rows * width, bytes_accessed=8 * rows * width, transcendentals=0),
    )(*parts)


def swiglu_backward(own, hidden, gate_act, up_act):
    rows, width = gate_act.shape
    half = rows // 2

    def kernel(facts_ref, near0, near1, cross0, cross1, gate_ref, up_ref, grad_gate_ref, grad_up_ref):
        crossed = facts_ref[S + 1] == 1
        for h, (near, cross) in enumerate(((near0, cross0), (near1, cross1))):
            here = slice(h * half, (h + 1) * half)
            value = jnp.where(crossed, cross[...].astype(F32), near[...].astype(F32))
            gate = gate_ref[here, :].astype(F32)
            sigmoid = jax.nn.sigmoid(gate)
            grad_up_ref[here, :] = (value * gate * sigmoid).astype(BF16)
            slope = sigmoid * (1.0 + gate * (1.0 - sigmoid))
            grad_gate_ref[here, :] = (value * up_ref[here, :].astype(F32) * slope).astype(BF16)

    return pl.pallas_call(
        kernel,
        in_specs=[SMEM] + [VMEM] * 6,
        out_specs=[VMEM] * 2,
        out_shape=[jax.ShapeDtypeStruct((rows, width), BF16)] * 2,
        compiler_params=params(16),
        cost_estimate=pl.CostEstimate(flops=10 * rows * width, bytes_accessed=10 * rows * width, transcendentals=rows * width),
    )(own, *hidden[0], *hidden[1], gate_act, up_act)


def on_device(grad_out, down_q, scales, gate_act, up_act):
    c = lax.axis_index("c")
    own = lax.dynamic_index_in_dim(jnp.asarray(facts()), lax.axis_index(ALL), 0, keepdims=False)

    near_own = dequantize(down_q, scales)
    near_other = shift(near_own, "c", C, 1)
    cut = 4 * BLOCK
    cross_own = [shift(near_own[:cut], "xh", XH, 1)]

    rows = grad_out.shape[0] // 2
    to = lambda k: [(i * C, (i + k) % Z * C) for i in range(Z)] + [(i * C + 1, (i - k) % Z * C + 1) for i in range(Z)]
    here = jnp.concatenate([grad_out, shift(grad_out, "c", C, 1)], 1)
    here, _ = lax.optimization_barrier((here, near_own))
    two = lax.ppermute(here, ("z", "c"), to(2))
    one = lax.ppermute(here, ("z", "c"), to(1))
    last, one = lax.optimization_barrier((near_own[cut:], one))
    cross_own.append(shift(last, "xh", XH, 1))
    two, cross_own[0] = lax.optimization_barrier((two, cross_own[0]))
    three = lax.ppermute(two, ("z", "c"), to(1))
    far = lax.ppermute(lax.dynamic_slice_in_dim(two, c * rows, rows, 0), ("z", "c"), to(2))
    cross_own, far, three = lax.optimization_barrier((jnp.concatenate(cross_own, 0), far, three))
    tokens = [here, one, two, three]
    cross_other = shift(cross_own, "c", C, 1)

    lhs, *near = product_y(own, tokens, far, near_own, near_other)
    near_y = [near[0]] + [shift(near[d], "y", Y, d) for d in range(1, Y)]
    sent = product_xl(lhs, cross_own, cross_other, 1)
    kept = product_xl(lhs, cross_own, cross_other, 0)
    cross = add_xl(kept, [shift(part, "xl", XL, 1) for part in sent])
    cross_parts = [cross[0]] + [shift(cross[d], "y", Y, d) for d in range(1, Y)]
    kept, sent = add_y(near_y)
    near_parts = [kept, shift(sent, "xl", XL, 1)]

    sums = [add_last(near_parts), add_last(cross_parts)]
    hidden = [[lax.ppermute(sums[r], ALL, home_pairs(r, h)) for h in range(2)] for r in range(2)]
    return tuple(swiglu_backward(own, hidden, gate_act, up_act))


def solution(mesh):
    fine = Mesh(mesh.devices.reshape(Z, XH, XL, Y, C), ALL)
    spec = P(FSDP, TP)
    return jax.shard_map(
        on_device, mesh=fine, in_specs=(spec,) * 5, out_specs=(spec, spec), check_vma=False
    )
```

```python
import numpy as np
import jax
import jax.numpy as jnp
from jax import lax
from jax.experimental import pallas as pl
from jax.experimental.pallas import tpu as pltpu
from jax.sharding import Mesh, PartitionSpec as P

BLOCK = 128
Z, XH, XL, Y, C = 8, 2, 2, 4, 2
S = XL * Y
FSDP = ("z", "xh")
TP = ("xl", "y", "c")
ALL = FSDP + TP
BF16, F32 = jnp.bfloat16, jnp.float32
VMEM = pl.BlockSpec(memory_space=pltpu.VMEM)
SMEM = pl.BlockSpec(memory_space=pltpu.SMEM)

NUMBER = (
    ((2, 5, 6, 1, 4, 0, 3, 7), (7, 3, 2, 4, 6, 1, 5, 0)),
    ((0, 5, 4, 6, 1, 7, 2, 3), (7, 3, 1, 4, 2, 5, 6, 0)),
    ((4, 2, 7, 0, 6, 1, 5, 3), (7, 5, 1, 4, 3, 2, 0, 6)),
    ((1, 5, 6, 4, 3, 7, 2, 0), (0, 5, 2, 1, 4, 6, 3, 7)),
    ((6, 4, 1, 7, 3, 0, 5, 2), (1, 0, 7, 4, 6, 2, 5, 3)),
    ((1, 3, 2, 7, 4, 6, 0, 5), (4, 6, 7, 0, 1, 3, 2, 5)),
    ((5, 4, 2, 6, 1, 0, 3, 7), (7, 5, 2, 1, 6, 4, 3, 0)),
    ((1, 0, 2, 4, 5, 7, 6, 3), (1, 0, 6, 4, 2, 5, 3, 7)),
)


def number_of(z, s, c):
    return NUMBER[z][c][s]


def half_of(number, c):
    return c if number in (0, 7) else (number - 1) % 2


def device_index(z, xh, s, c):
    return ((z * XH + xh) * S + s) * C + c


def home_pairs(j):
    pairs = []
    for z in range(Z):
        for xh in range(XH):
            for s in range(S):
                for c in range(C):
                    number = number_of(z, s, c)
                    away = (number + 1) // 2
                    to = (z - away if c == 0 else z + away) % Z
                    pairs.append((device_index(z, xh, s, c), device_index(to, xh, z, j ^ half_of(number, c))))
    return pairs


def facts():
    rows = []
    for z in range(Z):
        for xh in range(XH):
            for xl in range(XL):
                for y in range(Y):
                    for c in range(C):
                        place = [0] * S
                        for s in range(S):
                            place[number_of(z, s, c)] = ((s // Y) ^ xl) * Y + (s % Y - y) % Y
                        rows.append(place + [c, half_of(number_of(z, xl * Y + y, c), c) ^ xh])
    return np.array(rows, np.int32)


def shift(x, axis, size, by):
    return lax.ppermute(x, axis, [(i, (i + by) % size) for i in range(size)])


def dequantize(values, scales):
    rows, cols = values.shape
    grid = values.astype(F32).reshape(rows // BLOCK, BLOCK, cols // BLOCK, BLOCK)
    grid = grid * scales.astype(F32)[:, None, :, None]
    return grid.reshape(rows, cols).astype(BF16)


DIMS = (((1,), (1,)), ((), ()))


def times(lhs, w_own, w_other):
    half = lhs.shape[1] // 2
    total = lax.dot_general(lhs[:, :half], w_own, DIMS, preferred_element_type=F32)
    total += lax.dot_general(lhs[:, half:], w_other, DIMS, preferred_element_type=F32)
    return total.astype(BF16)


def params(mib):
    return pltpu.CompilerParams(vmem_limit_bytes=mib * 2**20)


def times_pieces(lhs, w_refs):
    count = len(w_refs) // 2
    return jnp.concatenate([times(lhs, w_refs[i][...], w_refs[count + i][...]) for i in range(count)], 1)


def product_send(own, tokens, far, weights):
    rows, depth = far.shape
    width = sum(w.shape[0] for w in weights) // 2
    count = len(weights)

    def kernel(facts_ref, t0, t1, t2, t3, far_ref, *refs):
        w_refs, lhs_ref, send_refs = refs[:count], refs[count], refs[count + 1 :]
        lhs_ref[facts_ref[0]] = t0[pl.ds(pl.multiple_of(facts_ref[S] * rows, rows), rows), :]
        for i, ref in enumerate((t1, t2, t3)):
            for h in range(2):
                lhs_ref[facts_ref[1 + 2 * i + h]] = ref[h * rows : (h + 1) * rows, :]
        lhs_ref[facts_ref[7]] = far_ref[...]
        total = times_pieces(lhs_ref[Y:].reshape(Y * rows, depth), w_refs)
        for d in range(Y):
            send_refs[d // 2][d % 2] = total[d * rows : (d + 1) * rows]

    return pl.pallas_call(
        kernel,
        in_specs=[SMEM] + [VMEM] * (5 + count),
        out_specs=[VMEM] * 3,
        out_shape=[jax.ShapeDtypeStruct((S, rows, depth), BF16)]
        + [jax.ShapeDtypeStruct((2, rows, width), BF16)] * 2,
        compiler_params=params(32),
        cost_estimate=pl.CostEstimate(flops=S * rows * depth * width, bytes_accessed=7 * 2**20, transcendentals=0),
    )(own, *tokens, far, *weights)


def product_y(lhs, w_own, w_other):
    _, rows, depth = lhs.shape
    width = w_own.shape[0]

    def kernel(lhs_ref, w_own_ref, w_other_ref, *out_refs):
        for e in range(2):
            total = times(lhs_ref[Y * e : Y * e + Y].reshape(Y * rows, depth), w_own_ref[...], w_other_ref[...])
            for d in range(Y):
                out_refs[d][e] = total[d * rows : (d + 1) * rows]

    return pl.pallas_call(
        kernel,
        in_specs=[VMEM] * 3,
        out_specs=[VMEM] * Y,
        out_shape=[jax.ShapeDtypeStruct((2, rows, width), BF16)] * Y,
        compiler_params=params(16),
        cost_estimate=pl.CostEstimate(flops=2 * S * rows * depth * width, bytes_accessed=6 * 2**20, transcendentals=0),
    )(lhs, w_own, w_other)


def product_keep(lhs, weights):
    _, rows, depth = lhs.shape
    width = sum(w.shape[0] for w in weights) // 2
    count = len(weights)

    def kernel(lhs_ref, *refs):
        total = times_pieces(lhs_ref[...].reshape(Y * rows, depth), refs[:count])
        for d in range(Y):
            refs[count + d // 2][d % 2] = total[d * rows : (d + 1) * rows]

    whole = lambda *shape: pl.BlockSpec(shape, lambda i: (0,) * len(shape))
    return pl.pallas_call(
        kernel,
        grid=(1,),
        in_specs=[whole(Y, rows, depth)] + [whole(*w.shape) for w in weights],
        out_specs=[whole(2, rows, width)] * 2,
        out_shape=[jax.ShapeDtypeStruct((2, rows, width), BF16)] * 2,
        compiler_params=params(16),
        cost_estimate=pl.CostEstimate(flops=S * rows * depth * width, bytes_accessed=4 * 2**20, transcendentals=0),
    )(lhs, *weights)


def add_y(parts):
    _, rows, width = parts[0].shape

    def kernel(*refs):
        for e in range(2):
            total = refs[0][e].astype(F32)
            for ref in refs[1:Y]:
                total += ref[e].astype(F32)
            refs[Y + e][...] = total.astype(BF16)

    return pl.pallas_call(
        kernel,
        in_specs=[VMEM] * Y,
        out_specs=[VMEM] * 2,
        out_shape=[jax.ShapeDtypeStruct((rows, width), BF16)] * 2,
        compiler_params=params(16),
        cost_estimate=pl.CostEstimate(flops=2 * Y * rows * width, bytes_accessed=4 * (Y + 1) * rows * width, transcendentals=0),
    )(*parts)


def add_xl(kept, received):
    _, rows, width = kept[0].shape

    def kernel(*refs):
        kept_refs, received_refs, out_refs = refs[:2], refs[2:4], refs[4:]
        for d in range(Y):
            total = kept_refs[d // 2][d % 2].astype(F32) + received_refs[d // 2][d % 2].astype(F32)
            out_refs[d][...] = total.astype(BF16)

    return pl.pallas_call(
        kernel,
        in_specs=[VMEM] * 4,
        out_specs=[VMEM] * Y,
        out_shape=[jax.ShapeDtypeStruct((rows, width), BF16)] * Y,
        compiler_params=params(16),
        cost_estimate=pl.CostEstimate(flops=Y * rows * width, bytes_accessed=6 * Y * rows * width, transcendentals=0),
    )(*kept, *received)


def add_last(own, near_parts, cross_parts):
    rows, width = near_parts[0].shape
    count = len(near_parts)

    def kernel(facts_ref, *refs):
        sums = []
        for parts in (refs[:count], refs[count : count + Y]):
            total = parts[0][...].astype(F32)
            for ref in parts[1:]:
                total += ref[...].astype(F32)
            sums.append(total)
        straight = facts_ref[S + 1] == 0
        refs[count + Y][...] = jnp.where(straight, sums[0], sums[1]).astype(BF16)
        refs[count + Y + 1][...] = jnp.where(straight, sums[1], sums[0]).astype(BF16)

    return pl.pallas_call(
        kernel,
        in_specs=[SMEM] + [VMEM] * (count + Y),
        out_specs=[VMEM] * 2,
        out_shape=[jax.ShapeDtypeStruct((rows, width), BF16)] * 2,
        compiler_params=params(16),
        cost_estimate=pl.CostEstimate(flops=8 * rows * width, bytes_accessed=16 * rows * width, transcendentals=0),
    )(own, *near_parts, *cross_parts)


def swiglu_backward(own, hidden, gate_act, up_act):
    rows, width = gate_act.shape
    half = rows // 2

    def kernel(facts_ref, first, second, gate_ref, up_ref, grad_gate_ref, grad_up_ref):
        flip = facts_ref[S] == 1
        for h, (straight, crossed) in enumerate(((first, second), (second, first))):
            here = slice(h * half, (h + 1) * half)
            value = jnp.where(flip, crossed[...].astype(F32), straight[...].astype(F32))
            gate = gate_ref[here, :].astype(F32)
            sigmoid = jax.nn.sigmoid(gate)
            grad_up_ref[here, :] = (value * gate * sigmoid).astype(BF16)
            slope = sigmoid * (1.0 + gate * (1.0 - sigmoid))
            grad_gate_ref[here, :] = (value * up_ref[here, :].astype(F32) * slope).astype(BF16)

    return pl.pallas_call(
        kernel,
        in_specs=[SMEM] + [VMEM] * 4,
        out_specs=[VMEM] * 2,
        out_shape=[jax.ShapeDtypeStruct((rows, width), BF16)] * 2,
        compiler_params=params(16),
        cost_estimate=pl.CostEstimate(flops=10 * rows * width, bytes_accessed=10 * rows * width, transcendentals=rows * width),
    )(own, *hidden, gate_act, up_act)


def on_device(grad_out, down_q, scales, gate_act, up_act):
    c = lax.axis_index("c")
    own = lax.dynamic_index_in_dim(jnp.asarray(facts()), lax.axis_index(ALL), 0, keepdims=False)

    near_own = dequantize(down_q, scales)
    near_other = shift(near_own, "c", C, 1)
    cut = 4 * BLOCK
    cross_own = [shift(near_own[:cut], "xh", XH, 1)]

    rows = grad_out.shape[0] // 2
    to = lambda k: [(i * C, (i + k) % Z * C) for i in range(Z)] + [(i * C + 1, (i - k) % Z * C + 1) for i in range(Z)]
    here = jnp.concatenate([grad_out, shift(grad_out, "c", C, 1)], 1)
    here, _ = lax.optimization_barrier((here, near_own))
    two = lax.ppermute(here, ("z", "c"), to(2))
    one = lax.ppermute(here, ("z", "c"), to(1))
    last, one = lax.optimization_barrier((near_own[cut:], one))
    cross_own.append(shift(last, "xh", XH, 1))
    two, cross_own[0] = lax.optimization_barrier((two, cross_own[0]))
    three = lax.ppermute(two, ("z", "c"), to(1))
    far = lax.ppermute(lax.dynamic_slice_in_dim(two, c * rows, rows, 0), ("z", "c"), to(2))
    tokens = [here, one, two, three]
    weights = cross_own + [shift(part, "c", C, 1) for part in cross_own]

    lhs, *sent = product_send(own, tokens, far, weights)
    near = product_y(lhs, near_own, near_other)
    near_y = [near[0]] + [shift(near[d], "y", Y, d) for d in range(1, Y)]
    kept = product_keep(lhs, weights)
    cross = add_xl(kept, [shift(part, "xl", XL, 1) for part in sent])
    cross_parts = [cross[0]] + [shift(cross[d], "y", Y, d) for d in range(1, Y)]
    kept, sent = add_y(near_y)
    near_parts = [kept, shift(sent, "xl", XL, 1)]

    sums = add_last(own, near_parts, cross_parts)
    hidden = [lax.ppermute(sums[j], ALL, home_pairs(j)) for j in range(2)]
    return tuple(swiglu_backward(own, hidden, gate_act, up_act))


def solution(mesh):
    fine = Mesh(mesh.devices.reshape(Z, XH, XL, Y, C), ALL)
    spec = P(FSDP, TP)
    return jax.shard_map(
        on_device, mesh=fine, in_specs=(spec,) * 5, out_specs=(spec, spec), check_vma=False
    )
```

```python
import numpy as np
import jax
import jax.numpy as jnp
from jax import lax
from jax.experimental import pallas as pl
from jax.experimental.pallas import tpu as pltpu
from jax.sharding import Mesh, PartitionSpec as P

BLOCK = 128
Z, XH, XL, Y, C = 8, 2, 2, 4, 2
S = XL * Y
FSDP = ("z", "xh")
TP = ("xl", "y", "c")
ALL = FSDP + TP
BF16, F32 = jnp.bfloat16, jnp.float32
VMEM = pl.BlockSpec(memory_space=pltpu.VMEM)
SMEM = pl.BlockSpec(memory_space=pltpu.SMEM)

NUMBER = (
    ((5, 1, 6, 2, 0, 3, 7, 4), (5, 1, 6, 2, 7, 3, 0, 4)),
    ((1, 5, 2, 6, 7, 3, 0, 4), (1, 5, 2, 6, 0, 3, 7, 4)),
    ((5, 1, 6, 2, 0, 3, 7, 4), (5, 1, 6, 2, 7, 3, 0, 4)),
    ((1, 5, 2, 6, 7, 3, 0, 4), (1, 5, 2, 6, 0, 3, 7, 4)),
    ((5, 1, 6, 2, 0, 3, 7, 4), (5, 1, 6, 2, 7, 3, 0, 4)),
    ((1, 5, 2, 6, 7, 3, 0, 4), (1, 5, 2, 6, 0, 3, 7, 4)),
    ((5, 1, 6, 2, 0, 3, 7, 4), (5, 1, 6, 2, 7, 3, 0, 4)),
    ((1, 5, 2, 6, 7, 3, 0, 4), (1, 5, 2, 6, 0, 3, 7, 4)),
)


def number_of(z, s, c):
    return NUMBER[z][c][s]


def half_of(number, c):
    return c if number in (0, 7) else (number - 1) % 2


def device_index(z, xh, s, c):
    return ((z * XH + xh) * S + s) * C + c


def home_pairs(j):
    pairs = []
    for z in range(Z):
        for xh in range(XH):
            for s in range(S):
                for c in range(C):
                    number = number_of(z, s, c)
                    away = (number + 1) // 2
                    to = (z - away if c == 0 else z + away) % Z
                    pairs.append((device_index(z, xh, s, c), device_index(to, xh, z, j ^ half_of(number, c))))
    return pairs


def facts():
    rows = []
    for z in range(Z):
        for xh in range(XH):
            for xl in range(XL):
                for y in range(Y):
                    for c in range(C):
                        place = [0] * S
                        for s in range(S):
                            place[number_of(z, s, c)] = ((s // Y) ^ xl) * Y + (s % Y - y) % Y
                        rows.append(place + [c, half_of(number_of(z, xl * Y + y, c), c) ^ xh])
    return np.array(rows, np.int32)


def shift(x, axis, size, by):
    return lax.ppermute(x, axis, [(i, (i + by) % size) for i in range(size)])


def dequantize(values, scales):
    rows, cols = values.shape
    grid = values.astype(F32).reshape(rows // BLOCK, BLOCK, cols // BLOCK, BLOCK)
    grid = grid * scales.astype(F32)[:, None, :, None]
    return grid.reshape(rows, cols).astype(BF16)


DIMS = (((1,), (1,)), ((), ()))


def times(lhs, w_own, w_other):
    half = lhs.shape[1] // 2
    total = lax.dot_general(lhs[:, :half], w_own, DIMS, preferred_element_type=F32)
    total += lax.dot_general(lhs[:, half:], w_other, DIMS, preferred_element_type=F32)
    return total.astype(BF16)


def params(mib):
    return pltpu.CompilerParams(vmem_limit_bytes=mib * 2**20)


def times_pieces(lhs, w_refs):
    count = len(w_refs) // 2
    return jnp.concatenate([times(lhs, w_refs[i][...], w_refs[count + i][...]) for i in range(count)], 1)


def product_send(own, tokens, far, weights):
    rows, depth = far.shape
    width = sum(w.shape[0] for w in weights) // 2
    count = len(weights)

    def kernel(facts_ref, t0, t1, t2, t3, far_ref, *refs):
        w_refs, lhs_ref, send_refs = refs[:count], refs[count], refs[count + 1 :]
        lhs_ref[facts_ref[0]] = t0[pl.ds(pl.multiple_of(facts_ref[S] * rows, rows), rows), :]
        for i, ref in enumerate((t1, t2, t3)):
            for h in range(2):
                lhs_ref[facts_ref[1 + 2 * i + h]] = ref[h * rows : (h + 1) * rows, :]
        lhs_ref[facts_ref[7]] = far_ref[...]
        total = times_pieces(lhs_ref[Y:].reshape(Y * rows, depth), w_refs)
        for d in range(Y):
            send_refs[d // 2][d % 2] = total[d * rows : (d + 1) * rows]

    return pl.pallas_call(
        kernel,
        in_specs=[SMEM] + [VMEM] * (5 + count),
        out_specs=[VMEM] * 3,
        out_shape=[jax.ShapeDtypeStruct((S, rows, depth), BF16)]
        + [jax.ShapeDtypeStruct((2, rows, width), BF16)] * 2,
        compiler_params=params(32),
        cost_estimate=pl.CostEstimate(flops=S * rows * depth * width, bytes_accessed=7 * 2**20, transcendentals=0),
    )(own, *tokens, far, *weights)


def product_y(lhs, w_own, w_other):
    _, rows, depth = lhs.shape
    width = w_own.shape[0]

    def kernel(lhs_ref, w_own_ref, w_other_ref, *out_refs):
        for e in range(2):
            total = times(lhs_ref[Y * e : Y * e + Y].reshape(Y * rows, depth), w_own_ref[...], w_other_ref[...])
            for d in range(Y):
                out_refs[d][e] = total[d * rows : (d + 1) * rows]

    return pl.pallas_call(
        kernel,
        in_specs=[VMEM] * 3,
        out_specs=[VMEM] * Y,
        out_shape=[jax.ShapeDtypeStruct((2, rows, width), BF16)] * Y,
        compiler_params=params(16),
        cost_estimate=pl.CostEstimate(flops=2 * S * rows * depth * width, bytes_accessed=6 * 2**20, transcendentals=0),
    )(lhs, w_own, w_other)


def product_keep(lhs, weights):
    _, rows, depth = lhs.shape
    width = sum(w.shape[0] for w in weights) // 2
    count = len(weights)

    def kernel(lhs_ref, *refs):
        total = times_pieces(lhs_ref[...].reshape(Y * rows, depth), refs[:count])
        for d in range(Y):
            refs[count + d // 2][d % 2] = total[d * rows : (d + 1) * rows]

    whole = lambda *shape: pl.BlockSpec(shape, lambda i: (0,) * len(shape))
    return pl.pallas_call(
        kernel,
        grid=(1,),
        in_specs=[whole(Y, rows, depth)] + [whole(*w.shape) for w in weights],
        out_specs=[whole(2, rows, width)] * 2,
        out_shape=[jax.ShapeDtypeStruct((2, rows, width), BF16)] * 2,
        compiler_params=params(16),
        cost_estimate=pl.CostEstimate(flops=S * rows * depth * width, bytes_accessed=4 * 2**20, transcendentals=0),
    )(lhs, *weights)


def add_y(parts):
    _, rows, width = parts[0].shape

    def kernel(*refs):
        for e in range(2):
            total = refs[0][e].astype(F32)
            for ref in refs[1:Y]:
                total += ref[e].astype(F32)
            refs[Y + e][...] = total.astype(BF16)

    return pl.pallas_call(
        kernel,
        in_specs=[VMEM] * Y,
        out_specs=[VMEM] * 2,
        out_shape=[jax.ShapeDtypeStruct((rows, width), BF16)] * 2,
        compiler_params=params(16),
        cost_estimate=pl.CostEstimate(flops=2 * Y * rows * width, bytes_accessed=4 * (Y + 1) * rows * width, transcendentals=0),
    )(*parts)


def add_xl(kept, received):
    _, rows, width = kept[0].shape

    def kernel(*refs):
        kept_refs, received_refs, out_refs = refs[:2], refs[2:4], refs[4:]
        for d in range(Y):
            total = kept_refs[d // 2][d % 2].astype(F32) + received_refs[d // 2][d % 2].astype(F32)
            out_refs[d][...] = total.astype(BF16)

    return pl.pallas_call(
        kernel,
        in_specs=[VMEM] * 4,
        out_specs=[VMEM] * Y,
        out_shape=[jax.ShapeDtypeStruct((rows, width), BF16)] * Y,
        compiler_params=params(16),
        cost_estimate=pl.CostEstimate(flops=Y * rows * width, bytes_accessed=6 * Y * rows * width, transcendentals=0),
    )(*kept, *received)


def add_last(own, near_parts, cross_parts):
    rows, width = near_parts[0].shape
    count = len(near_parts)

    def kernel(facts_ref, *refs):
        sums = []
        for parts in (refs[:count], refs[count : count + Y]):
            total = parts[0][...].astype(F32)
            for ref in parts[1:]:
                total += ref[...].astype(F32)
            sums.append(total)
        straight = facts_ref[S + 1] == 0
        refs[count + Y][...] = jnp.where(straight, sums[0], sums[1]).astype(BF16)
        refs[count + Y + 1][...] = jnp.where(straight, sums[1], sums[0]).astype(BF16)

    return pl.pallas_call(
        kernel,
        in_specs=[SMEM] + [VMEM] * (count + Y),
        out_specs=[VMEM] * 2,
        out_shape=[jax.ShapeDtypeStruct((rows, width), BF16)] * 2,
        compiler_params=params(16),
        cost_estimate=pl.CostEstimate(flops=8 * rows * width, bytes_accessed=16 * rows * width, transcendentals=0),
    )(own, *near_parts, *cross_parts)


def swiglu_backward(own, hidden, gate_act, up_act):
    rows, width = gate_act.shape
    half = rows // 2

    def kernel(facts_ref, first, second, gate_ref, up_ref, grad_gate_ref, grad_up_ref):
        flip = facts_ref[S] == 1
        for h, (straight, crossed) in enumerate(((first, second), (second, first))):
            here = slice(h * half, (h + 1) * half)
            value = jnp.where(flip, crossed[...].astype(F32), straight[...].astype(F32))
            gate = gate_ref[here, :].astype(F32)
            sigmoid = jax.nn.sigmoid(gate)
            grad_up_ref[here, :] = (value * gate * sigmoid).astype(BF16)
            slope = sigmoid * (1.0 + gate * (1.0 - sigmoid))
            grad_gate_ref[here, :] = (value * up_ref[here, :].astype(F32) * slope).astype(BF16)

    return pl.pallas_call(
        kernel,
        in_specs=[SMEM] + [VMEM] * 4,
        out_specs=[VMEM] * 2,
        out_shape=[jax.ShapeDtypeStruct((rows, width), BF16)] * 2,
        compiler_params=params(16),
        cost_estimate=pl.CostEstimate(flops=10 * rows * width, bytes_accessed=10 * rows * width, transcendentals=rows * width),
    )(own, *hidden, gate_act, up_act)


def on_device(grad_out, down_q, scales, gate_act, up_act):
    c = lax.axis_index("c")
    own = lax.dynamic_index_in_dim(jnp.asarray(facts()), lax.axis_index(ALL), 0, keepdims=False)

    near_own = dequantize(down_q, scales)
    near_other = shift(near_own, "c", C, 1)
    cut = 6 * BLOCK
    cross_own = [shift(near_own[:cut], "xh", XH, 1)]

    rows = grad_out.shape[0] // 2
    to = lambda k: [(i * C, (i + k) % Z * C) for i in range(Z)] + [(i * C + 1, (i - k) % Z * C + 1) for i in range(Z)]
    here = jnp.concatenate([grad_out, shift(grad_out, "c", C, 1)], 1)
    here, _ = lax.optimization_barrier((here, near_own))
    two = lax.ppermute(here, ("z", "c"), to(2))
    one = lax.ppermute(here, ("z", "c"), to(1))
    last, one = lax.optimization_barrier((near_own[cut:], one))
    cross_own.append(shift(last, "xh", XH, 1))
    two, cross_own[0] = lax.optimization_barrier((two, cross_own[0]))
    three = lax.ppermute(two, ("z", "c"), to(1))
    far = lax.ppermute(lax.dynamic_slice_in_dim(two, c * rows, rows, 0), ("z", "c"), to(2))
    tokens = [here, one, two, three]
    weights = cross_own + [shift(part, "c", C, 1) for part in cross_own]

    lhs, *sent = product_send(own, tokens, far, weights)
    near = product_y(lhs, near_own, near_other)
    near_y = [near[0]] + [shift(near[d], "y", Y, d) for d in range(1, Y)]
    kept = product_keep(lhs, weights)
    cross = add_xl(kept, [shift(part, "xl", XL, 1) for part in sent])
    cross_parts = [cross[0]] + [shift(cross[d], "y", Y, d) for d in range(1, Y)]
    kept, sent = add_y(near_y)
    near_parts = [kept, shift(sent, "xl", XL, 1)]

    sums = add_last(own, near_parts, cross_parts)
    hidden = [lax.ppermute(sums[j], ALL, home_pairs(j)) for j in range(2)]
    return tuple(swiglu_backward(own, hidden, gate_act, up_act))


def solution(mesh):
    fine = Mesh(mesh.devices.reshape(Z, XH, XL, Y, C), ALL)
    spec = P(FSDP, TP)
    return jax.shard_map(
        on_device, mesh=fine, in_specs=(spec,) * 5, out_specs=(spec, spec), check_vma=False
    )
```

```python
import numpy as np
import jax
import jax.numpy as jnp
from jax import lax
from jax.experimental import pallas as pl
from jax.experimental.pallas import tpu as pltpu
from jax.sharding import Mesh, PartitionSpec as P

BLOCK = 128
Z, XH, XL, Y, C = 8, 2, 2, 4, 2
S = XL * Y
FSDP = ("z", "xh")
TP = ("xl", "y", "c")
ALL = FSDP + TP
BF16, F32 = jnp.bfloat16, jnp.float32
VMEM = pl.BlockSpec(memory_space=pltpu.VMEM)
SMEM = pl.BlockSpec(memory_space=pltpu.SMEM)

NUMBER = (
    ((5, 1, 6, 2, 0, 3, 7, 4), (5, 1, 6, 2, 7, 3, 0, 4)),
    ((1, 5, 2, 6, 7, 3, 0, 4), (1, 5, 2, 6, 0, 3, 7, 4)),
    ((5, 1, 6, 2, 0, 3, 7, 4), (5, 1, 6, 2, 7, 3, 0, 4)),
    ((1, 5, 2, 6, 7, 3, 0, 4), (1, 5, 2, 6, 0, 3, 7, 4)),
    ((5, 1, 6, 2, 0, 3, 7, 4), (5, 1, 6, 2, 7, 3, 0, 4)),
    ((1, 5, 2, 6, 7, 3, 0, 4), (1, 5, 2, 6, 0, 3, 7, 4)),
    ((5, 1, 6, 2, 0, 3, 7, 4), (5, 1, 6, 2, 7, 3, 0, 4)),
    ((1, 5, 2, 6, 7, 3, 0, 4), (1, 5, 2, 6, 0, 3, 7, 4)),
)


def number_of(z, s, c):
    return NUMBER[z][c][s]


def half_of(number, c):
    return c if number in (0, 7) else (number - 1) % 2


def device_index(z, xh, s, c):
    return ((z * XH + xh) * S + s) * C + c


def home_pairs(j):
    pairs = []
    for z in range(Z):
        for xh in range(XH):
            for s in range(S):
                for c in range(C):
                    number = number_of(z, s, c)
                    away = (number + 1) // 2
                    to = (z - away if c == 0 else z + away) % Z
                    pairs.append((device_index(z, xh, s, c), device_index(to, xh, z, j ^ half_of(number, c))))
    return pairs


def facts():
    rows = []
    for z in range(Z):
        for xh in range(XH):
            for xl in range(XL):
                for y in range(Y):
                    for c in range(C):
                        place = [0] * S
                        for s in range(S):
                            place[number_of(z, s, c)] = ((s // Y) ^ xl) * Y + (s % Y - y) % Y
                        rows.append(place + [c, half_of(number_of(z, xl * Y + y, c), c) ^ xh])
    return np.array(rows, np.int32)


def shift(x, axis, size, by):
    return lax.ppermute(x, axis, [(i, (i + by) % size) for i in range(size)])


def dequantize(values, scales):
    rows, cols = values.shape
    grid = values.astype(F32).reshape(rows // BLOCK, BLOCK, cols // BLOCK, BLOCK)
    grid = grid * scales.astype(F32)[:, None, :, None]
    return grid.reshape(rows, cols).astype(BF16)


DIMS = (((1,), (1,)), ((), ()))


def times(lhs, w_own, w_other):
    half = lhs.shape[1] // 2
    total = lax.dot_general(lhs[:, :half], w_own, DIMS, preferred_element_type=F32)
    total += lax.dot_general(lhs[:, half:], w_other, DIMS, preferred_element_type=F32)
    return total.astype(BF16)


def params(mib):
    return pltpu.CompilerParams(vmem_limit_bytes=mib * 2**20)


def times_pieces(lhs, w_refs):
    count = len(w_refs) // 2
    return jnp.concatenate([times(lhs, w_refs[i][...], w_refs[count + i][...]) for i in range(count)], 1)


def product_send(own, tokens, far, weights):
    rows, depth = far.shape
    width = sum(w.shape[0] for w in weights) // 2
    count = len(weights)

    def kernel(facts_ref, t0, t1, t2, t3, far_ref, *refs):
        w_refs, lhs_ref, send_refs = refs[:count], refs[count], refs[count + 1 :]
        lhs_ref[facts_ref[0]] = t0[pl.ds(pl.multiple_of(facts_ref[S] * rows, rows), rows), :]
        for i, ref in enumerate((t1, t2, t3)):
            for h in range(2):
                lhs_ref[facts_ref[1 + 2 * i + h]] = ref[h * rows : (h + 1) * rows, :]
        lhs_ref[facts_ref[7]] = far_ref[...]
        total = times_pieces(lhs_ref[Y:].reshape(Y * rows, depth), w_refs)
        for d in range(Y):
            send_refs[d // 2][d % 2] = total[d * rows : (d + 1) * rows]

    return pl.pallas_call(
        kernel,
        in_specs=[SMEM] + [VMEM] * (5 + count),
        out_specs=[VMEM] * 3,
        out_shape=[jax.ShapeDtypeStruct((S, rows, depth), BF16)]
        + [jax.ShapeDtypeStruct((2, rows, width), BF16)] * 2,
        compiler_params=params(32),
        cost_estimate=pl.CostEstimate(flops=S * rows * depth * width, bytes_accessed=7 * 2**20, transcendentals=0),
    )(own, *tokens, far, *weights)


def product_y(lhs, w_own, w_other):
    _, rows, depth = lhs.shape
    width = w_own.shape[0]

    def kernel(lhs_ref, w_own_ref, w_other_ref, *out_refs):
        for e in range(2):
            total = times(lhs_ref[Y * e : Y * e + Y].reshape(Y * rows, depth), w_own_ref[...], w_other_ref[...])
            for d in range(Y):
                out_refs[d][e] = total[d * rows : (d + 1) * rows]

    return pl.pallas_call(
        kernel,
        in_specs=[VMEM] * 3,
        out_specs=[VMEM] * Y,
        out_shape=[jax.ShapeDtypeStruct((2, rows, width), BF16)] * Y,
        compiler_params=params(16),
        cost_estimate=pl.CostEstimate(flops=2 * S * rows * depth * width, bytes_accessed=6 * 2**20, transcendentals=0),
    )(lhs, w_own, w_other)


def product_keep(lhs, weights):
    _, rows, depth = lhs.shape
    width = sum(w.shape[0] for w in weights) // 2
    count = len(weights)

    def kernel(lhs_ref, *refs):
        total = times_pieces(lhs_ref[...].reshape(Y * rows, depth), refs[:count])
        for d in range(Y):
            refs[count + d // 2][d % 2] = total[d * rows : (d + 1) * rows]

    whole = lambda *shape: pl.BlockSpec(shape, lambda i: (0,) * len(shape))
    return pl.pallas_call(
        kernel,
        grid=(1,),
        in_specs=[whole(Y, rows, depth)] + [whole(*w.shape) for w in weights],
        out_specs=[whole(2, rows, width)] * 2,
        out_shape=[jax.ShapeDtypeStruct((2, rows, width), BF16)] * 2,
        compiler_params=params(16),
        cost_estimate=pl.CostEstimate(flops=S * rows * depth * width, bytes_accessed=4 * 2**20, transcendentals=0),
    )(lhs, *weights)


def add_y(parts):
    _, rows, width = parts[0].shape

    def kernel(*refs):
        for e in range(2):
            total = refs[0][e].astype(F32)
            for ref in refs[1:Y]:
                total += ref[e].astype(F32)
            refs[Y + e][...] = total.astype(BF16)

    return pl.pallas_call(
        kernel,
        in_specs=[VMEM] * Y,
        out_specs=[VMEM] * 2,
        out_shape=[jax.ShapeDtypeStruct((rows, width), BF16)] * 2,
        compiler_params=params(16),
        cost_estimate=pl.CostEstimate(flops=2 * Y * rows * width, bytes_accessed=4 * (Y + 1) * rows * width, transcendentals=0),
    )(*parts)


def add_xl(kept, received):
    _, rows, width = kept[0].shape

    def kernel(*refs):
        kept_refs, received_refs, out_refs = refs[:2], refs[2:4], refs[4:]
        for d in range(Y):
            total = kept_refs[d // 2][d % 2].astype(F32) + received_refs[d // 2][d % 2].astype(F32)
            out_refs[d][...] = total.astype(BF16)

    return pl.pallas_call(
        kernel,
        in_specs=[VMEM] * 4,
        out_specs=[VMEM] * Y,
        out_shape=[jax.ShapeDtypeStruct((rows, width), BF16)] * Y,
        compiler_params=params(16),
        cost_estimate=pl.CostEstimate(flops=Y * rows * width, bytes_accessed=6 * Y * rows * width, transcendentals=0),
    )(*kept, *received)


def add_last(own, near_parts, cross_parts):
    rows, width = near_parts[0].shape
    count = len(near_parts)

    def kernel(facts_ref, *refs):
        sums = []
        for parts in (refs[:count], refs[count : count + Y]):
            total = parts[0][...].astype(F32)
            for ref in parts[1:]:
                total += ref[...].astype(F32)
            sums.append(total)
        straight = facts_ref[S + 1] == 0
        refs[count + Y][...] = jnp.where(straight, sums[0], sums[1]).astype(BF16)
        refs[count + Y + 1][...] = jnp.where(straight, sums[1], sums[0]).astype(BF16)

    return pl.pallas_call(
        kernel,
        in_specs=[SMEM] + [VMEM] * (count + Y),
        out_specs=[VMEM] * 2,
        out_shape=[jax.ShapeDtypeStruct((rows, width), BF16)] * 2,
        compiler_params=params(16),
        cost_estimate=pl.CostEstimate(flops=8 * rows * width, bytes_accessed=16 * rows * width, transcendentals=0),
    )(own, *near_parts, *cross_parts)


def slopes(gate_act, up_act):
    rows, width = gate_act.shape

    def kernel(gate_ref, up_ref, for_up_ref, for_gate_ref):
        gate = gate_ref[...].astype(F32)
        sigmoid = jax.nn.sigmoid(gate)
        for_up_ref[...] = gate * sigmoid
        for_gate_ref[...] = up_ref[...].astype(F32) * (sigmoid * (1.0 + gate * (1.0 - sigmoid)))

    return pl.pallas_call(
        kernel,
        in_specs=[VMEM] * 2,
        out_specs=[VMEM] * 2,
        out_shape=[jax.ShapeDtypeStruct((rows, width), F32)] * 2,
        compiler_params=params(16),
        cost_estimate=pl.CostEstimate(flops=8 * rows * width, bytes_accessed=12 * rows * width, transcendentals=rows * width),
    )(gate_act, up_act)


def gradients(own, hidden, for_up, for_gate):
    rows, width = for_up.shape
    half = rows // 2

    def kernel(facts_ref, first, second, for_up_ref, for_gate_ref, grad_gate_ref, grad_up_ref):
        flip = facts_ref[S] == 1
        for h, (straight, crossed) in enumerate(((first, second), (second, first))):
            here = slice(h * half, (h + 1) * half)
            value = jnp.where(flip, crossed[...].astype(F32), straight[...].astype(F32))
            grad_up_ref[here, :] = (value * for_up_ref[here, :]).astype(BF16)
            grad_gate_ref[here, :] = (value * for_gate_ref[here, :]).astype(BF16)

    return pl.pallas_call(
        kernel,
        in_specs=[SMEM] + [VMEM] * 4,
        out_specs=[VMEM] * 2,
        out_shape=[jax.ShapeDtypeStruct((rows, width), BF16)] * 2,
        compiler_params=params(16),
        cost_estimate=pl.CostEstimate(flops=2 * rows * width, bytes_accessed=12 * rows * width, transcendentals=0),
    )(own, *hidden, for_up, for_gate)


def on_device(grad_out, down_q, scales, gate_act, up_act):
    c = lax.axis_index("c")
    own = lax.dynamic_index_in_dim(jnp.asarray(facts()), lax.axis_index(ALL), 0, keepdims=False)

    near_own = dequantize(down_q, scales)
    near_other = shift(near_own, "c", C, 1)
    cut = 6 * BLOCK
    cross_own = [shift(near_own[:cut], "xh", XH, 1)]

    rows = grad_out.shape[0] // 2
    to = lambda k: [(i * C, (i + k) % Z * C) for i in range(Z)] + [(i * C + 1, (i - k) % Z * C + 1) for i in range(Z)]
    here = jnp.concatenate([grad_out, shift(grad_out, "c", C, 1)], 1)
    here, _ = lax.optimization_barrier((here, near_own))
    two = lax.ppermute(here, ("z", "c"), to(2))
    one = lax.ppermute(here, ("z", "c"), to(1))
    last, one = lax.optimization_barrier((near_own[cut:], one))
    cross_own.append(shift(last, "xh", XH, 1))
    three = lax.ppermute(two, ("z", "c"), to(1))
    gated, cross_own[0] = lax.optimization_barrier((two, cross_own[0]))
    far = lax.ppermute(lax.dynamic_slice_in_dim(gated, c * rows, rows, 0), ("z", "c"), to(2))
    tokens = [here, one, two, three]
    weights = cross_own + [shift(part, "c", C, 1) for part in cross_own]

    lhs, *sent = product_send(own, tokens, far, weights)
    near = product_y(lhs, near_own, near_other)
    near_y = [near[0]] + [shift(near[d], "y", Y, d) for d in range(1, Y)]
    kept = product_keep(lhs, weights)
    cross = add_xl(kept, [shift(part, "xl", XL, 1) for part in sent])
    cross_parts = [cross[0]] + [shift(cross[d], "y", Y, d) for d in range(1, Y)]
    kept, sent = add_y(near_y)
    near_parts = [kept, shift(sent, "xl", XL, 1)]

    sums = add_last(own, near_parts, cross_parts)
    hidden = [lax.ppermute(sums[j], ALL, home_pairs(j)) for j in range(2)]
    return tuple(gradients(own, hidden, *slopes(gate_act, up_act)))


def solution(mesh):
    fine = Mesh(mesh.devices.reshape(Z, XH, XL, Y, C), ALL)
    spec = P(FSDP, TP)
    return jax.shard_map(
        on_device, mesh=fine, in_specs=(spec,) * 5, out_specs=(spec, spec), check_vma=False
    )
```

```python
import numpy as np
import jax
import jax.numpy as jnp
from jax import lax
from jax.experimental import pallas as pl
from jax.experimental.pallas import tpu as pltpu
from jax.sharding import Mesh, PartitionSpec as P

BLOCK = 128
Z, XH, XL, Y, C = 8, 2, 2, 4, 2
S = XL * Y
FSDP = ("z", "xh")
TP = ("xl", "y", "c")
ALL = FSDP + TP
BF16, F32 = jnp.bfloat16, jnp.float32
VMEM = pl.BlockSpec(memory_space=pltpu.VMEM)
SMEM = pl.BlockSpec(memory_space=pltpu.SMEM)

NUMBER = (
    ((5, 1, 6, 2, 0, 3, 7, 4), (5, 1, 6, 2, 7, 3, 0, 4)),
    ((1, 5, 2, 6, 7, 3, 0, 4), (1, 5, 2, 6, 0, 3, 7, 4)),
    ((5, 1, 6, 2, 0, 3, 7, 4), (5, 1, 6, 2, 7, 3, 0, 4)),
    ((1, 5, 2, 6, 7, 3, 0, 4), (1, 5, 2, 6, 0, 3, 7, 4)),
    ((5, 1, 6, 2, 0, 3, 7, 4), (5, 1, 6, 2, 7, 3, 0, 4)),
    ((1, 5, 2, 6, 7, 3, 0, 4), (1, 5, 2, 6, 0, 3, 7, 4)),
    ((5, 1, 6, 2, 0, 3, 7, 4), (5, 1, 6, 2, 7, 3, 0, 4)),
    ((1, 5, 2, 6, 7, 3, 0, 4), (1, 5, 2, 6, 0, 3, 7, 4)),
)


def number_of(z, s, c):
    return NUMBER[z][c][s]


def half_of(number, c):
    return c if number in (0, 7) else (number - 1) % 2


def device_index(z, xh, s, c):
    return ((z * XH + xh) * S + s) * C + c


def home_pairs(j):
    pairs = []
    for z in range(Z):
        for xh in range(XH):
            for s in range(S):
                for c in range(C):
                    number = number_of(z, s, c)
                    away = (number + 1) // 2
                    to = (z - away if c == 0 else z + away) % Z
                    pairs.append((device_index(z, xh, s, c), device_index(to, xh, z, j ^ half_of(number, c))))
    return pairs


def facts():
    rows = []
    for z in range(Z):
        for xh in range(XH):
            for xl in range(XL):
                for y in range(Y):
                    for c in range(C):
                        place = [0] * S
                        for s in range(S):
                            place[number_of(z, s, c)] = ((s // Y) ^ xl) * Y + (s % Y - y) % Y
                        rows.append(place + [c, half_of(number_of(z, xl * Y + y, c), c) ^ xh])
    return np.array(rows, np.int32)


def shift(x, axis, size, by):
    return lax.ppermute(x, axis, [(i, (i + by) % size) for i in range(size)])


def dequantize(values, scales):
    rows, cols = values.shape
    grid = values.astype(F32).reshape(rows // BLOCK, BLOCK, cols // BLOCK, BLOCK)
    grid = grid * scales.astype(F32)[:, None, :, None]
    return grid.reshape(rows, cols).astype(BF16)


DIMS = (((1,), (1,)), ((), ()))


def times(lhs, w_own, w_other):
    half = lhs.shape[1] // 2
    total = lax.dot_general(lhs[:, :half], w_own, DIMS, preferred_element_type=F32)
    total += lax.dot_general(lhs[:, half:], w_other, DIMS, preferred_element_type=F32)
    return total.astype(BF16)


def params(mib):
    return pltpu.CompilerParams(vmem_limit_bytes=mib * 2**20)


def times_pieces(lhs, w_refs):
    count = len(w_refs) // 2
    return jnp.concatenate([times(lhs, w_refs[i][...], w_refs[count + i][...]) for i in range(count)], 1)


def product_send(own, tokens, far, weights):
    rows, depth = far.shape
    width = sum(w.shape[0] for w in weights) // 2
    count = len(weights)

    def kernel(facts_ref, t0, t1, t2, t3, far_ref, *refs):
        w_refs, lhs_ref, send_refs = refs[:count], refs[count], refs[count + 1 :]
        lhs_ref[facts_ref[0]] = t0[pl.ds(pl.multiple_of(facts_ref[S] * rows, rows), rows), :]
        for i, ref in enumerate((t1, t2, t3)):
            for h in range(2):
                lhs_ref[facts_ref[1 + 2 * i + h]] = ref[h * rows : (h + 1) * rows, :]
        lhs_ref[facts_ref[7]] = far_ref[...]
        total = times_pieces(lhs_ref[Y:].reshape(Y * rows, depth), w_refs)
        for d in range(Y):
            send_refs[d // 2][d % 2] = total[d * rows : (d + 1) * rows]

    return pl.pallas_call(
        kernel,
        in_specs=[SMEM] + [VMEM] * (5 + count),
        out_specs=[VMEM] * 3,
        out_shape=[jax.ShapeDtypeStruct((S, rows, depth), BF16)]
        + [jax.ShapeDtypeStruct((2, rows, width), BF16)] * 2,
        compiler_params=params(32),
        cost_estimate=pl.CostEstimate(flops=S * rows * depth * width, bytes_accessed=7 * 2**20, transcendentals=0),
    )(own, *tokens, far, *weights)


def product_y(lhs, w_own, w_other):
    _, rows, depth = lhs.shape
    width = w_own.shape[0]

    def kernel(lhs_ref, w_own_ref, w_other_ref, *out_refs):
        for e in range(2):
            total = times(lhs_ref[Y * e : Y * e + Y].reshape(Y * rows, depth), w_own_ref[...], w_other_ref[...])
            for d in range(Y):
                out_refs[d][e] = total[d * rows : (d + 1) * rows]

    return pl.pallas_call(
        kernel,
        in_specs=[VMEM] * 3,
        out_specs=[VMEM] * Y,
        out_shape=[jax.ShapeDtypeStruct((2, rows, width), BF16)] * Y,
        compiler_params=params(16),
        cost_estimate=pl.CostEstimate(flops=2 * S * rows * depth * width, bytes_accessed=6 * 2**20, transcendentals=0),
    )(lhs, w_own, w_other)


def product_keep(lhs, weights):
    _, rows, depth = lhs.shape
    width = sum(w.shape[0] for w in weights) // 2
    count = len(weights)

    def kernel(lhs_ref, *refs):
        total = times_pieces(lhs_ref[...].reshape(Y * rows, depth), refs[:count])
        for d in range(Y):
            refs[count + d // 2][d % 2] = total[d * rows : (d + 1) * rows]

    whole = lambda *shape: pl.BlockSpec(shape, lambda i: (0,) * len(shape))
    return pl.pallas_call(
        kernel,
        grid=(1,),
        in_specs=[whole(Y, rows, depth)] + [whole(*w.shape) for w in weights],
        out_specs=[whole(2, rows, width)] * 2,
        out_shape=[jax.ShapeDtypeStruct((2, rows, width), BF16)] * 2,
        compiler_params=params(16),
        cost_estimate=pl.CostEstimate(flops=S * rows * depth * width, bytes_accessed=4 * 2**20, transcendentals=0),
    )(lhs, *weights)


def add_y(parts):
    _, rows, width = parts[0].shape

    def kernel(*refs):
        for e in range(2):
            total = refs[0][e].astype(F32)
            for ref in refs[1:Y]:
                total += ref[e].astype(F32)
            refs[Y + e][...] = total.astype(BF16)

    return pl.pallas_call(
        kernel,
        in_specs=[VMEM] * Y,
        out_specs=[VMEM] * 2,
        out_shape=[jax.ShapeDtypeStruct((rows, width), BF16)] * 2,
        compiler_params=params(16),
        cost_estimate=pl.CostEstimate(flops=2 * Y * rows * width, bytes_accessed=4 * (Y + 1) * rows * width, transcendentals=0),
    )(*parts)


def add_xl(kept, received):
    _, rows, width = kept[0].shape

    def kernel(*refs):
        kept_refs, received_refs, out_refs = refs[:2], refs[2:4], refs[4:]
        for d in range(Y):
            total = kept_refs[d // 2][d % 2].astype(F32) + received_refs[d // 2][d % 2].astype(F32)
            out_refs[d][...] = total.astype(BF16)

    return pl.pallas_call(
        kernel,
        in_specs=[VMEM] * 4,
        out_specs=[VMEM] * Y,
        out_shape=[jax.ShapeDtypeStruct((rows, width), BF16)] * Y,
        compiler_params=params(16),
        cost_estimate=pl.CostEstimate(flops=Y * rows * width, bytes_accessed=6 * Y * rows * width, transcendentals=0),
    )(*kept, *received)


def add_last(own, near_parts, cross_parts):
    rows, width = near_parts[0].shape
    count = len(near_parts)

    def kernel(facts_ref, *refs):
        sums = []
        for parts in (refs[:count], refs[count : count + Y]):
            total = parts[0][...].astype(F32)
            for ref in parts[1:]:
                total += ref[...].astype(F32)
            sums.append(total)
        straight = facts_ref[S + 1] == 0
        refs[count + Y][...] = jnp.where(straight, sums[0], sums[1]).astype(BF16)
        refs[count + Y + 1][...] = jnp.where(straight, sums[1], sums[0]).astype(BF16)

    return pl.pallas_call(
        kernel,
        in_specs=[SMEM] + [VMEM] * (count + Y),
        out_specs=[VMEM] * 2,
        out_shape=[jax.ShapeDtypeStruct((rows, width), BF16)] * 2,
        compiler_params=params(16),
        cost_estimate=pl.CostEstimate(flops=8 * rows * width, bytes_accessed=16 * rows * width, transcendentals=0),
    )(own, *near_parts, *cross_parts)


def slopes(gate_act, up_act):
    rows, width = gate_act.shape

    def kernel(gate_ref, up_ref, for_up_ref, for_gate_ref):
        gate = gate_ref[...].astype(F32)
        sigmoid = jax.nn.sigmoid(gate)
        for_up_ref[...] = gate * sigmoid
        for_gate_ref[...] = up_ref[...].astype(F32) * (sigmoid * (1.0 + gate * (1.0 - sigmoid)))

    return pl.pallas_call(
        kernel,
        in_specs=[VMEM] * 2,
        out_specs=[VMEM] * 2,
        out_shape=[jax.ShapeDtypeStruct((rows, width), F32)] * 2,
        compiler_params=params(16),
        cost_estimate=pl.CostEstimate(flops=8 * rows * width, bytes_accessed=12 * rows * width, transcendentals=rows * width),
    )(gate_act, up_act)


def gradients(own, hidden, for_up, for_gate):
    rows, width = for_up.shape
    half = rows // 2

    def kernel(facts_ref, first, second, for_up_ref, for_gate_ref, grad_gate_ref, grad_up_ref):
        flip = facts_ref[S] == 1
        for h, (straight, crossed) in enumerate(((first, second), (second, first))):
            here = slice(h * half, (h + 1) * half)
            value = jnp.where(flip, crossed[...].astype(F32), straight[...].astype(F32))
            grad_up_ref[here, :] = (value * for_up_ref[here, :]).astype(BF16)
            grad_gate_ref[here, :] = (value * for_gate_ref[here, :]).astype(BF16)

    return pl.pallas_call(
        kernel,
        in_specs=[SMEM] + [VMEM] * 4,
        out_specs=[VMEM] * 2,
        out_shape=[jax.ShapeDtypeStruct((rows, width), BF16)] * 2,
        compiler_params=params(16),
        cost_estimate=pl.CostEstimate(flops=2 * rows * width, bytes_accessed=12 * rows * width, transcendentals=0),
    )(own, *hidden, for_up, for_gate)


def on_device(grad_out, down_q, scales, gate_act, up_act):
    c = lax.axis_index("c")
    own = lax.dynamic_index_in_dim(jnp.asarray(facts()), lax.axis_index(ALL), 0, keepdims=False)

    near_own = dequantize(down_q, scales)
    near_other = shift(near_own, "c", C, 1)
    cut = 5 * BLOCK
    cross_own = [shift(near_own[:cut], "xh", XH, 1)]

    rows = grad_out.shape[0] // 2
    to = lambda k: [(i * C, (i + k) % Z * C) for i in range(Z)] + [(i * C + 1, (i - k) % Z * C + 1) for i in range(Z)]
    here = jnp.concatenate([grad_out, shift(grad_out, "c", C, 1)], 1)
    here, _ = lax.optimization_barrier((here, near_own))
    two = lax.ppermute(here, ("z", "c"), to(2))
    one = lax.ppermute(here, ("z", "c"), to(1))
    last, one, cross_own[0] = lax.optimization_barrier((near_own[cut:], one, cross_own[0]))
    cross_own.append(shift(last, "xh", XH, 1))
    three = lax.ppermute(two, ("z", "c"), to(1))
    far = lax.ppermute(lax.dynamic_slice_in_dim(two, c * rows, rows, 0), ("z", "c"), to(2))
    tokens = [here, one, two, three]
    weights = cross_own + [shift(part, "c", C, 1) for part in cross_own]

    lhs, *sent = product_send(own, tokens, far, weights)
    near = product_y(lhs, near_own, near_other)
    near_y = [near[0]] + [shift(near[d], "y", Y, d) for d in range(1, Y)]
    kept = product_keep(lhs, weights)
    cross = add_xl(kept, [shift(part, "xl", XL, 1) for part in sent])
    cross_parts = [cross[0]] + [shift(cross[d], "y", Y, d) for d in range(1, Y)]
    kept, sent = add_y(near_y)
    near_parts = [kept, shift(sent, "xl", XL, 1)]

    sums = add_last(own, near_parts, cross_parts)
    hidden = [lax.ppermute(sums[j], ALL, home_pairs(j)) for j in range(2)]
    return tuple(gradients(own, hidden, *slopes(gate_act, up_act)))


def solution(mesh):
    fine = Mesh(mesh.devices.reshape(Z, XH, XL, Y, C), ALL)
    spec = P(FSDP, TP)
    return jax.shard_map(
        on_device, mesh=fine, in_specs=(spec,) * 5, out_specs=(spec, spec), check_vma=False
    )
```

```python
import numpy as np
import jax
import jax.numpy as jnp
from jax import lax
from jax.experimental import pallas as pl
from jax.experimental.pallas import tpu as pltpu
from jax.sharding import Mesh, PartitionSpec as P

BLOCK = 128
Z, XH, XL, Y, C = 8, 2, 2, 4, 2
S = XL * Y
FSDP = ("z", "xh")
TP = ("xl", "y", "c")
ALL = FSDP + TP
BF16, F32 = jnp.bfloat16, jnp.float32
VMEM = pl.BlockSpec(memory_space=pltpu.VMEM)
SMEM = pl.BlockSpec(memory_space=pltpu.SMEM)

NUMBER = (
    ((5, 1, 6, 2, 0, 3, 7, 4), (5, 1, 6, 2, 7, 3, 0, 4)),
    ((1, 5, 2, 6, 7, 3, 0, 4), (1, 5, 2, 6, 0, 3, 7, 4)),
    ((5, 1, 6, 2, 0, 3, 7, 4), (5, 1, 6, 2, 7, 3, 0, 4)),
    ((1, 5, 2, 6, 7, 3, 0, 4), (1, 5, 2, 6, 0, 3, 7, 4)),
    ((5, 1, 6, 2, 0, 3, 7, 4), (5, 1, 6, 2, 7, 3, 0, 4)),
    ((1, 5, 2, 6, 7, 3, 0, 4), (1, 5, 2, 6, 0, 3, 7, 4)),
    ((5, 1, 6, 2, 0, 3, 7, 4), (5, 1, 6, 2, 7, 3, 0, 4)),
    ((1, 5, 2, 6, 7, 3, 0, 4), (1, 5, 2, 6, 0, 3, 7, 4)),
)


def number_of(z, s, c):
    return NUMBER[z][c][s]


def half_of(number, c):
    return c if number in (0, 7) else (number - 1) % 2


def device_index(z, xh, s, c):
    return ((z * XH + xh) * S + s) * C + c


def home_pairs(j):
    pairs = []
    for z in range(Z):
        for xh in range(XH):
            for s in range(S):
                for c in range(C):
                    number = number_of(z, s, c)
                    away = (number + 1) // 2
                    to = (z - away if c == 0 else z + away) % Z
                    pairs.append((device_index(z, xh, s, c), device_index(to, xh, z, j ^ half_of(number, c))))
    return pairs


def facts():
    rows = []
    for z in range(Z):
        for xh in range(XH):
            for xl in range(XL):
                for y in range(Y):
                    for c in range(C):
                        place = [0] * S
                        for s in range(S):
                            place[number_of(z, s, c)] = ((s // Y) ^ xl) * Y + (s % Y - y) % Y
                        rows.append(place + [c, half_of(number_of(z, xl * Y + y, c), c) ^ xh])
    return np.array(rows, np.int32)


def shift(x, axis, size, by):
    return lax.ppermute(x, axis, [(i, (i + by) % size) for i in range(size)])


def dequantize(values, scales):
    rows, cols = values.shape
    grid = values.astype(F32).reshape(rows // BLOCK, BLOCK, cols // BLOCK, BLOCK)
    grid = grid * scales.astype(F32)[:, None, :, None]
    return grid.reshape(rows, cols).astype(BF16)


DIMS = (((1,), (1,)), ((), ()))


def times(lhs, w_own, w_other):
    half = lhs.shape[1] // 2
    total = lax.dot_general(lhs[:, :half], w_own, DIMS, preferred_element_type=F32)
    total += lax.dot_general(lhs[:, half:], w_other, DIMS, preferred_element_type=F32)
    return total.astype(BF16)


def params(mib):
    return pltpu.CompilerParams(vmem_limit_bytes=mib * 2**20)


def times_pieces(lhs, w_refs):
    count = len(w_refs) // 2
    return jnp.concatenate([times(lhs, w_refs[i][...], w_refs[count + i][...]) for i in range(count)], 1)


def product_send(own, tokens, far, weights):
    rows, depth = far.shape
    width = sum(w.shape[0] for w in weights) // 2
    count = len(weights)

    def kernel(facts_ref, t0, t1, t2, t3, far_ref, *refs):
        w_refs, lhs_ref, send_ref = refs[:count], refs[count], refs[count + 1]
        lhs_ref[facts_ref[0]] = t0[pl.ds(pl.multiple_of(facts_ref[S] * rows, rows), rows), :]
        for i, ref in enumerate((t1, t2, t3)):
            for h in range(2):
                lhs_ref[facts_ref[1 + 2 * i + h]] = ref[h * rows : (h + 1) * rows, :]
        lhs_ref[facts_ref[7]] = far_ref[...]
        total = times_pieces(lhs_ref[Y:].reshape(Y * rows, depth), w_refs)
        for d in range(Y):
            send_ref[d] = total[d * rows : (d + 1) * rows]

    return pl.pallas_call(
        kernel,
        in_specs=[SMEM] + [VMEM] * (5 + count),
        out_specs=[VMEM] * 2,
        out_shape=[jax.ShapeDtypeStruct((n, rows, w), BF16) for n, w in ((S, depth), (Y, width))],
        compiler_params=params(32),
        cost_estimate=pl.CostEstimate(flops=S * rows * depth * width, bytes_accessed=7 * 2**20, transcendentals=0),
    )(own, *tokens, far, *weights)


def product_y(lhs, w_own, w_other):
    _, rows, depth = lhs.shape
    width = w_own.shape[0]

    def kernel(lhs_ref, w_own_ref, w_other_ref, *out_refs):
        for e in range(2):
            total = times(lhs_ref[Y * e : Y * e + Y].reshape(Y * rows, depth), w_own_ref[...], w_other_ref[...])
            for d in range(Y):
                out_refs[d][e] = total[d * rows : (d + 1) * rows]

    return pl.pallas_call(
        kernel,
        in_specs=[VMEM] * 3,
        out_specs=[VMEM] * Y,
        out_shape=[jax.ShapeDtypeStruct((2, rows, width), BF16)] * Y,
        compiler_params=params(16),
        cost_estimate=pl.CostEstimate(flops=2 * S * rows * depth * width, bytes_accessed=6 * 2**20, transcendentals=0),
    )(lhs, w_own, w_other)


def product_keep(lhs, weights):
    _, rows, depth = lhs.shape
    width = sum(w.shape[0] for w in weights) // 2
    count = len(weights)

    def kernel(lhs_ref, *refs):
        total = times_pieces(lhs_ref[...].reshape(Y * rows, depth), refs[:count])
        for d in range(Y):
            refs[count + d // 2][d % 2] = total[d * rows : (d + 1) * rows]

    whole = lambda *shape: pl.BlockSpec(shape, lambda i: (0,) * len(shape))
    return pl.pallas_call(
        kernel,
        grid=(1,),
        in_specs=[whole(Y, rows, depth)] + [whole(*w.shape) for w in weights],
        out_specs=[whole(2, rows, width)] * 2,
        out_shape=[jax.ShapeDtypeStruct((2, rows, width), BF16)] * 2,
        compiler_params=params(16),
        cost_estimate=pl.CostEstimate(flops=S * rows * depth * width, bytes_accessed=4 * 2**20, transcendentals=0),
    )(lhs, *weights)


def add_y(parts):
    _, rows, width = parts[0].shape

    def kernel(*refs):
        for e in range(2):
            total = refs[0][e].astype(F32)
            for ref in refs[1:Y]:
                total += ref[e].astype(F32)
            refs[Y + e][...] = total.astype(BF16)

    return pl.pallas_call(
        kernel,
        in_specs=[VMEM] * Y,
        out_specs=[VMEM] * 2,
        out_shape=[jax.ShapeDtypeStruct((rows, width), BF16)] * 2,
        compiler_params=params(16),
        cost_estimate=pl.CostEstimate(flops=2 * Y * rows * width, bytes_accessed=4 * (Y + 1) * rows * width, transcendentals=0),
    )(*parts)


def add_xl(kept, received):
    _, rows, width = kept[0].shape

    def kernel(*refs):
        kept_refs, received_ref, out_refs = refs[:2], refs[2], refs[3:]
        for d in range(Y):
            total = kept_refs[d // 2][d % 2].astype(F32) + received_ref[d].astype(F32)
            out_refs[d][...] = total.astype(BF16)

    return pl.pallas_call(
        kernel,
        in_specs=[VMEM] * 3,
        out_specs=[VMEM] * Y,
        out_shape=[jax.ShapeDtypeStruct((rows, width), BF16)] * Y,
        compiler_params=params(16),
        cost_estimate=pl.CostEstimate(flops=Y * rows * width, bytes_accessed=6 * Y * rows * width, transcendentals=0),
    )(*kept, received)


def add_last(own, near_parts, cross_parts):
    rows, width = near_parts[0].shape
    count = len(near_parts)

    def kernel(facts_ref, *refs):
        sums = []
        for parts in (refs[:count], refs[count : count + Y]):
            total = parts[0][...].astype(F32)
            for ref in parts[1:]:
                total += ref[...].astype(F32)
            sums.append(total)
        straight = facts_ref[S + 1] == 0
        refs[count + Y][...] = jnp.where(straight, sums[0], sums[1]).astype(BF16)
        refs[count + Y + 1][...] = jnp.where(straight, sums[1], sums[0]).astype(BF16)

    return pl.pallas_call(
        kernel,
        in_specs=[SMEM] + [VMEM] * (count + Y),
        out_specs=[VMEM] * 2,
        out_shape=[jax.ShapeDtypeStruct((rows, width), BF16)] * 2,
        compiler_params=params(16),
        cost_estimate=pl.CostEstimate(flops=8 * rows * width, bytes_accessed=16 * rows * width, transcendentals=0),
    )(own, *near_parts, *cross_parts)


def slopes(gate_act, up_act):
    rows, width = gate_act.shape

    def kernel(gate_ref, up_ref, for_up_ref, for_gate_ref):
        gate = gate_ref[...].astype(F32)
        sigmoid = jax.nn.sigmoid(gate)
        for_up_ref[...] = gate * sigmoid
        for_gate_ref[...] = up_ref[...].astype(F32) * (sigmoid * (1.0 + gate * (1.0 - sigmoid)))

    return pl.pallas_call(
        kernel,
        in_specs=[VMEM] * 2,
        out_specs=[VMEM] * 2,
        out_shape=[jax.ShapeDtypeStruct((rows, width), F32)] * 2,
        compiler_params=params(16),
        cost_estimate=pl.CostEstimate(flops=8 * rows * width, bytes_accessed=12 * rows * width, transcendentals=rows * width),
    )(gate_act, up_act)


def gradients(own, hidden, for_up, for_gate):
    rows, width = for_up.shape
    half = rows // 2

    def kernel(facts_ref, first, second, for_up_ref, for_gate_ref, grad_gate_ref, grad_up_ref):
        flip = facts_ref[S] == 1
        for h, (straight, crossed) in enumerate(((first, second), (second, first))):
            here = slice(h * half, (h + 1) * half)
            value = jnp.where(flip, crossed[...].astype(F32), straight[...].astype(F32))
            grad_up_ref[here, :] = (value * for_up_ref[here, :]).astype(BF16)
            grad_gate_ref[here, :] = (value * for_gate_ref[here, :]).astype(BF16)

    return pl.pallas_call(
        kernel,
        in_specs=[SMEM] + [VMEM] * 4,
        out_specs=[VMEM] * 2,
        out_shape=[jax.ShapeDtypeStruct((rows, width), BF16)] * 2,
        compiler_params=params(16),
        cost_estimate=pl.CostEstimate(flops=2 * rows * width, bytes_accessed=12 * rows * width, transcendentals=0),
    )(own, *hidden, for_up, for_gate)


def on_device(grad_out, down_q, scales, gate_act, up_act):
    c = lax.axis_index("c")
    own = lax.dynamic_index_in_dim(jnp.asarray(facts()), lax.axis_index(ALL), 0, keepdims=False)

    near_own = dequantize(down_q, scales)
    near_other = shift(near_own, "c", C, 1)
    cut = 6 * BLOCK
    cross_own = [shift(near_own[:cut], "xh", XH, 1)]

    rows = grad_out.shape[0] // 2
    to = lambda k: [(i * C, (i + k) % Z * C) for i in range(Z)] + [(i * C + 1, (i - k) % Z * C + 1) for i in range(Z)]
    here = jnp.concatenate([grad_out, shift(grad_out, "c", C, 1)], 1)
    here, _ = lax.optimization_barrier((here, near_own))
    two = lax.ppermute(here, ("z", "c"), to(2))
    one = lax.ppermute(here, ("z", "c"), to(1))
    last, one = lax.optimization_barrier((near_own[cut:], one))
    cross_own.append(shift(last, "xh", XH, 1))
    three = lax.ppermute(two, ("z", "c"), to(1))
    gated, cross_own[0] = lax.optimization_barrier((two, cross_own[0]))
    far = lax.ppermute(lax.dynamic_slice_in_dim(gated, c * rows, rows, 0), ("z", "c"), to(2))
    tokens = [here, one, two, three]
    weights = cross_own + [shift(part, "c", C, 1) for part in cross_own]

    lhs, sent = product_send(own, tokens, far, weights)
    near = product_y(lhs, near_own, near_other)
    near_y = [near[0]] + [shift(near[d], "y", Y, d) for d in range(1, Y)]
    kept = product_keep(lhs, weights)
    cross = add_xl(kept, shift(sent, "xl", XL, 1))
    cross_parts = [cross[0]] + [shift(cross[d], "y", Y, d) for d in range(1, Y)]
    kept, sent = add_y(near_y)
    near_parts = [kept, shift(sent, "xl", XL, 1)]

    sums = add_last(own, near_parts, cross_parts)
    hidden = [lax.ppermute(sums[j], ALL, home_pairs(j)) for j in range(2)]
    return tuple(gradients(own, hidden, *slopes(gate_act, up_act)))


def solution(mesh):
    fine = Mesh(mesh.devices.reshape(Z, XH, XL, Y, C), ALL)
    spec = P(FSDP, TP)
    return jax.shard_map(
        on_device, mesh=fine, in_specs=(spec,) * 5, out_specs=(spec, spec), check_vma=False
    )
```

```python
import numpy as np
import jax
import jax.numpy as jnp
from jax import lax
from jax.experimental import pallas as pl
from jax.experimental.pallas import tpu as pltpu
from jax.sharding import Mesh, PartitionSpec as P

BLOCK = 128
Z, XH, XL, Y, C = 8, 2, 2, 4, 2
S = XL * Y
FSDP = ("z", "xh")
TP = ("xl", "y", "c")
ALL = FSDP + TP
BF16, F32 = jnp.bfloat16, jnp.float32
VMEM = pl.BlockSpec(memory_space=pltpu.VMEM)
SMEM = pl.BlockSpec(memory_space=pltpu.SMEM)

NUMBER = (
    ((5, 1, 6, 2, 0, 3, 7, 4), (5, 1, 6, 2, 7, 3, 0, 4)),
    ((1, 5, 2, 6, 7, 3, 0, 4), (1, 5, 2, 6, 0, 3, 7, 4)),
    ((5, 1, 6, 2, 0, 3, 7, 4), (5, 1, 6, 2, 7, 3, 0, 4)),
    ((1, 5, 2, 6, 7, 3, 0, 4), (1, 5, 2, 6, 0, 3, 7, 4)),
    ((5, 1, 6, 2, 0, 3, 7, 4), (5, 1, 6, 2, 7, 3, 0, 4)),
    ((1, 5, 2, 6, 7, 3, 0, 4), (1, 5, 2, 6, 0, 3, 7, 4)),
    ((5, 1, 6, 2, 0, 3, 7, 4), (5, 1, 6, 2, 7, 3, 0, 4)),
    ((1, 5, 2, 6, 7, 3, 0, 4), (1, 5, 2, 6, 0, 3, 7, 4)),
)


def number_of(z, s, c):
    return NUMBER[z][c][s]


def half_of(number, c):
    return c if number in (0, 7) else (number - 1) % 2


def device_index(z, xh, s, c):
    return ((z * XH + xh) * S + s) * C + c


def home_pairs(j):
    pairs = []
    for z in range(Z):
        for xh in range(XH):
            for s in range(S):
                for c in range(C):
                    number = number_of(z, s, c)
                    away = (number + 1) // 2
                    to = (z - away if c == 0 else z + away) % Z
                    pairs.append((device_index(z, xh, s, c), device_index(to, xh, z, j ^ half_of(number, c))))
    return pairs


def facts():
    rows = []
    for z in range(Z):
        for xh in range(XH):
            for xl in range(XL):
                for y in range(Y):
                    for c in range(C):
                        place = [0] * S
                        for s in range(S):
                            place[number_of(z, s, c)] = ((s // Y) ^ xl) * Y + (s % Y - y) % Y
                        rows.append(place + [c, half_of(number_of(z, xl * Y + y, c), c) ^ xh])
    return np.array(rows, np.int32)


def shift(x, axis, size, by):
    return lax.ppermute(x, axis, [(i, (i + by) % size) for i in range(size)])


def dequantize(values, scales):
    rows, cols = values.shape
    grid = values.astype(F32).reshape(rows // BLOCK, BLOCK, cols // BLOCK, BLOCK)
    grid = grid * scales.astype(F32)[:, None, :, None]
    return grid.reshape(rows, cols).astype(BF16)


DIMS = (((1,), (1,)), ((), ()))


def times(lhs, w_own, w_other):
    half = lhs.shape[1] // 2
    total = lax.dot_general(lhs[:, :half], w_own, DIMS, preferred_element_type=F32)
    total += lax.dot_general(lhs[:, half:], w_other, DIMS, preferred_element_type=F32)
    return total.astype(BF16)


def params(mib):
    return pltpu.CompilerParams(vmem_limit_bytes=mib * 2**20)


def times_pieces(lhs, w_refs):
    count = len(w_refs) // 2
    return jnp.concatenate([times(lhs, w_refs[i][...], w_refs[count + i][...]) for i in range(count)], 1)


def product_send(own, tokens, far, weights):
    rows, depth = far.shape
    width = sum(w.shape[0] for w in weights) // 2
    count = len(weights)

    def kernel(facts_ref, t0, t1, t2, t3, far_ref, *refs):
        w_refs, lhs_ref, send_refs = refs[:count], refs[count], refs[count + 1 :]
        lhs_ref[facts_ref[0]] = t0[pl.ds(pl.multiple_of(facts_ref[S] * rows, rows), rows), :]
        for i, ref in enumerate((t1, t2, t3)):
            for h in range(2):
                lhs_ref[facts_ref[1 + 2 * i + h]] = ref[h * rows : (h + 1) * rows, :]
        lhs_ref[facts_ref[7]] = far_ref[...]
        total = times_pieces(lhs_ref[Y:].reshape(Y * rows, depth), w_refs)
        for d in range(Y):
            send_refs[d // 2][d % 2] = total[d * rows : (d + 1) * rows]

    return pl.pallas_call(
        kernel,
        in_specs=[SMEM] + [VMEM] * (5 + count),
        out_specs=[VMEM] * 3,
        out_shape=[jax.ShapeDtypeStruct((S, rows, depth), BF16)]
        + [jax.ShapeDtypeStruct((2, rows, width), BF16)] * 2,
        compiler_params=params(32),
        cost_estimate=pl.CostEstimate(flops=S * rows * depth * width, bytes_accessed=7 * 2**20, transcendentals=0),
    )(own, *tokens, far, *weights)


def product_y(lhs, w_own, w_other):
    _, rows, depth = lhs.shape
    width = w_own.shape[0]

    def kernel(lhs_ref, w_own_ref, w_other_ref, *out_refs):
        for e in range(2):
            total = times(lhs_ref[Y * e : Y * e + Y].reshape(Y * rows, depth), w_own_ref[...], w_other_ref[...])
            for d in range(Y):
                out_refs[d][e] = total[d * rows : (d + 1) * rows]

    return pl.pallas_call(
        kernel,
        in_specs=[VMEM] * 3,
        out_specs=[VMEM] * Y,
        out_shape=[jax.ShapeDtypeStruct((2, rows, width), BF16)] * Y,
        compiler_params=params(16),
        cost_estimate=pl.CostEstimate(flops=2 * S * rows * depth * width, bytes_accessed=6 * 2**20, transcendentals=0),
    )(lhs, w_own, w_other)


def product_keep(lhs, weights):
    _, rows, depth = lhs.shape
    width = sum(w.shape[0] for w in weights) // 2
    count = len(weights)

    def kernel(lhs_ref, *refs):
        total = times_pieces(lhs_ref[...].reshape(Y * rows, depth), refs[:count])
        for d in range(Y):
            refs[count + d // 2][d % 2] = total[d * rows : (d + 1) * rows]

    whole = lambda *shape: pl.BlockSpec(shape, lambda i: (0,) * len(shape))
    return pl.pallas_call(
        kernel,
        grid=(1,),
        in_specs=[whole(Y, rows, depth)] + [whole(*w.shape) for w in weights],
        out_specs=[whole(2, rows, width)] * 2,
        out_shape=[jax.ShapeDtypeStruct((2, rows, width), BF16)] * 2,
        compiler_params=params(16),
        cost_estimate=pl.CostEstimate(flops=S * rows * depth * width, bytes_accessed=4 * 2**20, transcendentals=0),
    )(lhs, *weights)


def add_y(parts):
    _, rows, width = parts[0].shape

    def kernel(*refs):
        for e in range(2):
            total = refs[0][e].astype(F32)
            for ref in refs[1:Y]:
                total += ref[e].astype(F32)
            refs[Y + e][...] = total.astype(BF16)

    return pl.pallas_call(
        kernel,
        in_specs=[VMEM] * Y,
        out_specs=[VMEM] * 2,
        out_shape=[jax.ShapeDtypeStruct((rows, width), BF16)] * 2,
        compiler_params=params(16),
        cost_estimate=pl.CostEstimate(flops=2 * Y * rows * width, bytes_accessed=4 * (Y + 1) * rows * width, transcendentals=0),
    )(*parts)


def add_xl(kept, received):
    _, rows, width = kept[0].shape

    def kernel(*refs):
        kept_refs, received_refs, out_refs = refs[:2], refs[2:4], refs[4:]
        for d in range(Y):
            total = kept_refs[d // 2][d % 2].astype(F32) + received_refs[d // 2][d % 2].astype(F32)
            out_refs[d][...] = total.astype(BF16)

    return pl.pallas_call(
        kernel,
        in_specs=[VMEM] * 4,
        out_specs=[VMEM] * Y,
        out_shape=[jax.ShapeDtypeStruct((rows, width), BF16)] * Y,
        compiler_params=params(16),
        cost_estimate=pl.CostEstimate(flops=Y * rows * width, bytes_accessed=6 * Y * rows * width, transcendentals=0),
    )(*kept, *received)


def add_last(own, near_parts, cross_parts):
    rows, width = near_parts[0].shape
    count = len(near_parts)

    def kernel(facts_ref, *refs):
        sums = []
        for parts in (refs[:count], refs[count : count + Y]):
            total = parts[0][...].astype(F32)
            for ref in parts[1:]:
                total += ref[...].astype(F32)
            sums.append(total)
        straight = facts_ref[S + 1] == 0
        refs[count + Y][...] = jnp.where(straight, sums[0], sums[1]).astype(BF16)
        refs[count + Y + 1][...] = jnp.where(straight, sums[1], sums[0]).astype(BF16)

    return pl.pallas_call(
        kernel,
        in_specs=[SMEM] + [VMEM] * (count + Y),
        out_specs=[VMEM] * 2,
        out_shape=[jax.ShapeDtypeStruct((rows, width), BF16)] * 2,
        compiler_params=params(16),
        cost_estimate=pl.CostEstimate(flops=8 * rows * width, bytes_accessed=16 * rows * width, transcendentals=0),
    )(own, *near_parts, *cross_parts)


def slopes(gate_act, up_act):
    rows, width = gate_act.shape

    def kernel(gate_ref, up_ref, for_up_ref, for_gate_ref):
        gate = gate_ref[...].astype(F32)
        sigmoid = jax.nn.sigmoid(gate)
        for_up_ref[...] = gate * sigmoid
        for_gate_ref[...] = up_ref[...].astype(F32) * (sigmoid * (1.0 + gate * (1.0 - sigmoid)))

    return pl.pallas_call(
        kernel,
        in_specs=[VMEM] * 2,
        out_specs=[VMEM] * 2,
        out_shape=[jax.ShapeDtypeStruct((rows, width), F32)] * 2,
        compiler_params=params(16),
        cost_estimate=pl.CostEstimate(flops=8 * rows * width, bytes_accessed=12 * rows * width, transcendentals=rows * width),
    )(gate_act, up_act)


def gradients(own, hidden, for_up, for_gate):
    rows, width = for_up.shape
    half = rows // 2

    def kernel(facts_ref, first, second, for_up_ref, for_gate_ref, grad_gate_ref, grad_up_ref):
        flip = facts_ref[S] == 1
        for h, (straight, crossed) in enumerate(((first, second), (second, first))):
            here = slice(h * half, (h + 1) * half)
            value = jnp.where(flip, crossed[...].astype(F32), straight[...].astype(F32))
            grad_up_ref[here, :] = (value * for_up_ref[here, :]).astype(BF16)
            grad_gate_ref[here, :] = (value * for_gate_ref[here, :]).astype(BF16)

    return pl.pallas_call(
        kernel,
        in_specs=[SMEM] + [VMEM] * 4,
        out_specs=[VMEM] * 2,
        out_shape=[jax.ShapeDtypeStruct((rows, width), BF16)] * 2,
        compiler_params=params(16),
        cost_estimate=pl.CostEstimate(flops=2 * rows * width, bytes_accessed=12 * rows * width, transcendentals=0),
    )(own, *hidden, for_up, for_gate)


def on_device(grad_out, down_q, scales, gate_act, up_act):
    c = lax.axis_index("c")
    own = lax.dynamic_index_in_dim(jnp.asarray(facts()), lax.axis_index(ALL), 0, keepdims=False)

    near_own = dequantize(down_q, scales)
    near_other = shift(near_own, "c", C, 1)
    cut = 6 * BLOCK
    cross_own = [shift(near_own[:cut], "xh", XH, 1)]

    rows = grad_out.shape[0] // 2
    to = lambda k: [(i * C, (i + k) % Z * C) for i in range(Z)] + [(i * C + 1, (i - k) % Z * C + 1) for i in range(Z)]
    here = jnp.concatenate([grad_out, shift(grad_out, "c", C, 1)], 1)
    here, _ = lax.optimization_barrier((here, near_own))
    two = lax.ppermute(here, ("z", "c"), to(2))
    one = lax.ppermute(here, ("z", "c"), to(1))
    last, one = lax.optimization_barrier((near_own[cut:], one))
    cross_own.append(shift(last, "xh", XH, 1))
    three = lax.ppermute(two, ("z", "c"), to(1))
    far = lax.ppermute(lax.dynamic_slice_in_dim(two, c * rows, rows, 0), ("z", "c"), to(2))
    tokens = [here, one, two, three]
    weights = cross_own + [shift(part, "c", C, 1) for part in cross_own]

    lhs, *sent = product_send(own, tokens, far, weights)
    near = product_y(lhs, near_own, near_other)
    near_y = [near[0]] + [shift(near[d], "y", Y, d) for d in range(1, Y)]
    kept = product_keep(lhs, weights)
    cross = add_xl(kept, [shift(part, "xl", XL, 1) for part in sent])
    cross_parts = [cross[0]] + [shift(cross[d], "y", Y, d) for d in range(1, Y)]
    kept, sent = add_y(near_y)
    near_parts = [kept, shift(sent, "xl", XL, 1)]

    sums = add_last(own, near_parts, cross_parts)
    hidden = [lax.ppermute(sums[j], ALL, home_pairs(j)) for j in range(2)]
    return tuple(gradients(own, hidden, *slopes(gate_act, up_act)))


def solution(mesh):
    fine = Mesh(mesh.devices.reshape(Z, XH, XL, Y, C), ALL)
    spec = P(FSDP, TP)
    return jax.shard_map(
        on_device, mesh=fine, in_specs=(spec,) * 5, out_specs=(spec, spec), check_vma=False
    )
```
